32 devices in a mesh: req: 8 (over z, y), tp: 4 (over x, core).
Axes of the slice: x: 2, y: 2, z: 4, core: 2. Of those that a mesh axis runs over, the one named last changes fastest.
Arguments:
- tokens: bfloat16 [4096, 1536], P(('req', 'tp')), may hold values from -8 to 8
- attention_norm_gain: bfloat16 [1536], replicated, may hold values from 0.5 to 1.5
- expert_norm_gain: bfloat16 [1536], replicated, may hold values from 0.5 to 1.5
- query_projection: bfloat16 [1536, 1536], P(None, 'tp'), may hold values from -1 to 1
- key_projection: bfloat16 [1536, 512], P(None, 'tp'), may hold values from -1 to 1
- value_projection: bfloat16 [1536, 512], P(None, 'tp'), may hold values from -0.15625 to 0.15625
- attention_output_weight: bfloat16 [1536, 1536], P('tp'), may hold values from -0.15625 to 0.15625
- cached_keys: bfloat16 [32768, 512], P('req', 'tp'), may hold values from -6 to 6
- cached_values: bfloat16 [32768, 512], P('req', 'tp'), may hold values from -6 to 6
- token_request: int32 [8, 512], P('req'), may hold values from 0 to 3, never falling along the last dimension, each value on 1 to 256 neighbouring positions
- cached_request: int32 [8, 4096], P('req'), may hold values from 0 to 3, never falling along the last dimension, each value on 1 to 2048 neighbouring positions
- adapter_of_request: int32 [8, 4], P('req'), may hold values from 0 to 63
- adapter_table_row: int32 [64], replicated, may hold values from 0 to 63, each once
- adapter_down_maps: bfloat16 [64, 16, 1536], P('req'), may hold values from -0.15625 to 0.15625
- adapter_query_up: bfloat16 [64, 16, 1536], P('req', None, 'tp'), may hold values from -1.5 to 1.5
- adapter_value_up: bfloat16 [64, 16, 512], P('req', None, 'tp'), may hold values from -1.5 to 1.5
- routes: int32 [4096, 8], P('req'), may hold values from 0 to 31, all different within a row; in each aligned block of 128 rows (0 to 127, 128 to 255, ...) at most 34 rows name the same one
- routed_weight: float32 [4096, 8], P('req'), may hold values from 0.03 to 0.3
- expert_gate_weight: bfloat16 [32, 1536, 512], P('req', None, 'tp'), may hold values from -0.15625 to 0.15625
- expert_up_weight: bfloat16 [32, 1536, 512], P('req', None, 'tp'), may hold values from -0.15625 to 0.15625
- expert_down_weight: bfloat16 [32, 512, 1536], P('req', 'tp'), may hold values from -0.25 to 0.25
Outputs:
- mixed: bfloat16 [4096, 1536], P(('req', 'tp'))
The draws below stay inside these ranges and needn't reach their ends.
Inputs may be any that keep to these rules, and one draw needn't show every extreme that they name: `routes`: each row names 8 different experts; within each aligned block of 128 rows (the rows of one device) no expert is named by more than 34 rows, a bound that some block reaches. `token_request`: along each row the request numbers never fall; every request has 1 to 256 new tokens and one has exactly that many. `cached_request`: along each row the request numbers never fall; every request has 1 to 2048 cached tokens and one has exactly that many. `adapter_table_row`: each row number of the adapter tables appears once.
All inputs are finite; a program needn't handle non-finite values.
Results may differ from the reference program's by a relative error of at most 0.01.
Values may be sent and summed in bfloat16 or wider, within the bound.
A program may use at most 128 MiB of HBM per device.

```python
import math
import jax
import jax.numpy as jnp
import numpy as np
from jax import lax

MODEL_WIDTH = 1536
QUERY_HEADS = 24
KEY_VALUE_HEADS = 8
HEAD_SIZE = 64
EXPERTS = 32
FF_E = 512
TOP = 8
ADAPTER_RANK = 16
ADAPTER_COUNT = 64
GROUP_REQUESTS = 4
REQUEST_TOKENS = 512
CONTEXT_TOKENS = 4096
TOK_DEV = 128
TOKEN_TOTAL = 4096
EXP_CAP = 34
N_REQ = 8
N_TP = 4


def draw_tokens(key, part):
    noise = jax.random.normal(jax.random.fold_in(key, 1), (TOKEN_TOTAL, MODEL_WIDTH), jnp.float32)
    values = noise
    return jnp.clip(values, -8.0, 8.0).astype(jnp.bfloat16)


def draw_query_projection(key, part):
    drawn_weight = jax.random.normal(jax.random.fold_in(key, 3), (MODEL_WIDTH, QUERY_HEADS * HEAD_SIZE), jnp.float32) * MODEL_WIDTH ** (-0.5)
    return jnp.clip(drawn_weight, -1.0, 1.0).astype(jnp.bfloat16)


def draw_key_projection(key, part):
    drawn_weight = jax.random.normal(jax.random.fold_in(key, 4), (MODEL_WIDTH, KEY_VALUE_HEADS * HEAD_SIZE), jnp.float32) * MODEL_WIDTH ** (-0.5)
    return jnp.clip(drawn_weight, -1.0, 1.0).astype(jnp.bfloat16)


def plant(entries, rng, low, top_value):
    place = [jax.random.randint(jax.random.fold_in(rng, axis), (), 0, length) for axis, length in enumerate(entries.shape)]
    widest = entries.shape.index(max(entries.shape))
    beside = place[:widest] + [(place[widest] + 1) % entries.shape[widest]] + place[widest + 1:]
    return entries.at[tuple(place)].set(low).at[tuple(beside)].set(top_value)


def shard_levels(rng, shape, cuts, least, top_value):
    factor_of, own = 1.0, jax.random.fold_in(rng, 6)
    for dim, parts in cuts:
        steps = jnp.exp(jax.random.uniform(jax.random.fold_in(own, dim), (parts,), jnp.float32, least / len(cuts), top_value / len(cuts)))
        factor_of = factor_of * jnp.repeat(steps, shape[dim] // parts).reshape([-1 if axis == dim else 1 for axis in range(len(shape))])
    return factor_of


def length_profile(count, total, bound, skew):
    weights = [(1 << 20) // math.isqrt(standing ** skew) + 1 for standing in range(2, count + 1)]
    spare, given = total - bound - (count - 1), [1] * (count - 1)
    while spare > 0:
        movable = [i for i in range(count - 1) if given[i] < bound]
        pool, left = sum([weights[i] for i in movable]), spare
        for i in movable:
            more = min(bound - given[i], max(1, left * weights[i] // pool), spare)
            given[i] = given[i] + more
            spare = spare - more
    return np.array([bound] + given)


def ragged(own_key, count, total, bound, skew):
    if count == 2:
        one = jax.random.randint(own_key, (), max(1, total - bound), min(bound, total - 1) + 1)
        return jnp.stack([one, total - one])
    lengths = jnp.asarray(length_profile(count, total, bound, skew), jnp.int32)
    couples = (count - 1) // 2
    source_of, taker = lengths[1:1 + 2 * couples:2], lengths[2:2 + 2 * couples:2]
    room = jnp.minimum(source_of - 1, bound - taker)
    passed = jax.random.randint(jax.random.fold_in(own_key, 1), (couples,), 0, 1 << 20) % (room + 1)
    lengths = lengths.at[1:1 + 2 * couples:2].set(source_of - passed).at[2:2 + 2 * couples:2].set(taker + passed)
    return lengths[jax.random.permutation(jax.random.fold_in(own_key, 2), count)]


def deal_out(own_key, own, number, rows, number_of, top, most, lean):
    order = jax.random.permutation(own_key, number_of)
    crowded, usual = shares(number_of, rows * top, most, lean, True), shares(number_of, rows * top, most, lean, False)
    places = jnp.arange(number_of)

    def named(sizes, offset_by):
        used = int((sizes > 0).sum())
        fixed = max(1, used // 4)
        moved = fixed + (places - fixed + offset_by * (used - fixed)) % max(1, number_of - fixed)
        return jnp.zeros((number_of,), jnp.int32).at[order[jnp.where(places < fixed, places, moved)]].set(jnp.asarray(sizes, jnp.int32))

    sizes = jnp.where(number % 4 == 0, named(crowded, number // 4), named(usual, number - number // 4 - 1))
    mixed = jax.random.permutation(jax.random.fold_in(own, 3), number_of)
    source_of, taker = mixed[0:number_of // 2 * 2:2], mixed[1:number_of // 2 * 2:2]
    slack = jnp.minimum(sizes[source_of] - 1, most - sizes[taker]) // 2
    slack = jnp.where((source_of == order[0]) | (taker == order[0]) | (sizes[taker] == 0), 0, jnp.maximum(slack, 0))
    moved = jax.random.randint(jax.random.fold_in(own, 4), (number_of // 2,), 0, 1 << 20) % (slack + 1)
    sizes = sizes.at[source_of].add(-moved).at[taker].add(moved)
    items = jnp.searchsorted(jnp.cumsum(sizes), jnp.arange(rows * top), side="right").astype(jnp.int32)
    listing = items.reshape(top, rows).T
    listing = listing[jax.random.permutation(jax.random.fold_in(own, 1), rows)]
    offset_by = jax.random.randint(jax.random.fold_in(own, 2), (rows, 1), 0, top)
    return jnp.take_along_axis(listing, (jnp.arange(top)[None, :] + offset_by) % top, axis=1)


def shares(amount, total, reach, lean, full):
    portions = [(1 << 20) // math.isqrt(standing ** lean) + 1 for standing in range(1, amount + 1)]
    largest = reach if full else min(reach, max(-(-total // amount), total * portions[0] // sum(portions)))
    least = 1 if total - largest >= amount - 1 else 0
    given, rest = [largest] + [least] * (amount - 1), total - largest - least * (amount - 1)
    while rest > 0:
        free = [i for i in range(1, amount) if given[i] < largest] or [i for i in range(1, amount) if given[i] < reach]
        whole, left = sum([portions[i] for i in free]), rest
        for i in free:
            addition = min(reach - given[i], max(1, left * portions[i] // whole), rest)
            given[i] = given[i] + addition
            rest = rest - addition
    return np.array(given)


def normal_values(key, shape, width, limit, cuts=(), kind=jnp.bfloat16):
    values = width * jax.random.normal(key, shape, jnp.float32)
    if cuts:
        values = values * shard_levels(key, shape, cuts, -0.22, 0.18)
    return jnp.clip(values, -limit, limit).astype(kind)


def setup_inputs(seed: int = 0) -> dict:
    arg_keys = jax.random.split(jax.random.key(seed), 22)
    tokens = draw_tokens(jax.random.fold_in(arg_keys[21], 71), 0)
    attention_norm_gain = jnp.clip(1.0 + 0.1 * jax.random.normal(arg_keys[1], (MODEL_WIDTH,), jnp.float32), 0.5, 1.5).astype(jnp.bfloat16)
    expert_norm_gain = jnp.clip(1.0 + 0.1 * jax.random.normal(arg_keys[2], (MODEL_WIDTH,), jnp.float32), 0.5, 1.5).astype(jnp.bfloat16)
    query_projection = draw_query_projection(jax.random.fold_in(arg_keys[21], 71), 0)
    key_projection = draw_key_projection(jax.random.fold_in(arg_keys[21], 71), 0)
    value_projection = normal_values(arg_keys[5], (MODEL_WIDTH, KEY_VALUE_HEADS * HEAD_SIZE), MODEL_WIDTH ** -0.5, 0.15625, ((1, 4),))
    attention_output_weight = normal_values(arg_keys[6], (QUERY_HEADS * HEAD_SIZE, MODEL_WIDTH), (QUERY_HEADS * HEAD_SIZE) ** -0.5, 0.15625, ((0, 4),))
    cached_keys = normal_values(arg_keys[7], (N_REQ * CONTEXT_TOKENS, KEY_VALUE_HEADS * HEAD_SIZE), 1.0, 6.0, ((0, 8), (1, 4)))
    cached_values = normal_values(arg_keys[8], (N_REQ * CONTEXT_TOKENS, KEY_VALUE_HEADS * HEAD_SIZE), 1.0, 6.0, ((0, 8), (1, 4)))
    token_request = jax.vmap(lambda own: jnp.searchsorted(jnp.cumsum(ragged(own, GROUP_REQUESTS, REQUEST_TOKENS, REQUEST_TOKENS // 2, 2)), jnp.arange(REQUEST_TOKENS), side="right"))(jax.random.split(arg_keys[9], N_REQ)).reshape((N_REQ, REQUEST_TOKENS)).astype(jnp.int32)
    cached_request = jax.vmap(lambda own: jnp.searchsorted(jnp.cumsum(ragged(own, GROUP_REQUESTS, CONTEXT_TOKENS, CONTEXT_TOKENS // 2, 2)), jnp.arange(CONTEXT_TOKENS), side="right"))(jax.random.split(arg_keys[10], N_REQ)).reshape((N_REQ, CONTEXT_TOKENS)).astype(jnp.int32)
    adapter_of_request = plant(jax.random.randint(arg_keys[11], (N_REQ, GROUP_REQUESTS), 0, ADAPTER_COUNT), jax.random.fold_in(arg_keys[11], 1), 0, ADAPTER_COUNT - 1).astype(jnp.int32)
    adapter_table_row = jax.random.permutation(arg_keys[12], ADAPTER_COUNT).astype(jnp.int32)
    adapter_down_maps = normal_values(arg_keys[13], (ADAPTER_COUNT, ADAPTER_RANK, MODEL_WIDTH), MODEL_WIDTH ** -0.5, 0.15625, ((0, 8),))
    adapter_query_up = normal_values(arg_keys[14], (ADAPTER_COUNT, ADAPTER_RANK, QUERY_HEADS * HEAD_SIZE), ADAPTER_RANK ** -0.5, 1.5, ((0, 8), (2, 4)))
    adapter_value_up = normal_values(arg_keys[15], (ADAPTER_COUNT, ADAPTER_RANK, KEY_VALUE_HEADS * HEAD_SIZE), ADAPTER_RANK ** -0.5, 1.5, ((0, 8), (2, 4)))
    routes_keys = jax.random.split(jax.random.fold_in(arg_keys[16], 1), TOKEN_TOTAL // TOK_DEV)
    routes_turns = jax.random.permutation(jax.random.fold_in(arg_keys[16], 3), TOKEN_TOTAL // TOK_DEV)
    routes = jax.vmap(lambda own, number: deal_out(jax.random.fold_in(arg_keys[16], 2), own, number, TOK_DEV, EXPERTS, TOP, EXP_CAP, 0))(routes_keys, routes_turns).reshape((TOKEN_TOTAL, TOP))
    routed_weight = jnp.clip(jnp.exp(math.log(0.3) - 2.3025852 * jax.random.uniform(arg_keys[17], (TOKEN_TOTAL, TOP), jnp.float32) ** shard_levels(arg_keys[17], (TOKEN_TOTAL, TOP), ((0, 8),), -0.2, 0.2)), 0.03, 0.3)
    expert_gate_weight = normal_values(arg_keys[18], (EXPERTS, MODEL_WIDTH, FF_E), MODEL_WIDTH ** -0.5, 0.15625, ((0, 8), (2, 4)))
    expert_up_weight = normal_values(arg_keys[19], (EXPERTS, MODEL_WIDTH, FF_E), MODEL_WIDTH ** -0.5, 0.15625, ((0, 8), (2, 4)))
    expert_down_weight = normal_values(arg_keys[20], (EXPERTS, FF_E, MODEL_WIDTH), FF_E ** -0.5, 0.25, ((0, 8), (1, 4)))
    return {"tokens": tokens, "attention_norm_gain": attention_norm_gain, "expert_norm_gain": expert_norm_gain, "query_projection": query_projection, "key_projection": key_projection, "value_projection": value_projection, "attention_output_weight": attention_output_weight, "cached_keys": cached_keys, "cached_values": cached_values, "token_request": token_request, "cached_request": cached_request, "adapter_of_request": adapter_of_request, "adapter_table_row": adapter_table_row, "adapter_down_maps": adapter_down_maps, "adapter_query_up": adapter_query_up, "adapter_value_up": adapter_value_up, "routes": routes, "routed_weight": routed_weight, "expert_gate_weight": expert_gate_weight, "expert_up_weight": expert_up_weight, "expert_down_weight": expert_down_weight}


norm_eps = 1e-05
rope_theta = 10000.0

def rms_norm(row_block, gain_row):
    values = row_block.astype(jnp.float32)
    inv_rms = lax.rsqrt(lax.optimization_barrier(jnp.mean(values * values, axis=-1, keepdims=True)) + norm_eps)
    return (values * inv_rms * gain_row.astype(jnp.float32)).astype(jnp.bfloat16)

def apply_rotation(vectors, token_places, head_count):
    row_count = vectors.shape[0]
    head_width = vectors.shape[1] // head_count
    half_width = head_width // 2
    shaped = vectors.reshape(row_count, head_count, head_width)
    spacing = jnp.arange(half_width).astype(jnp.float32) / half_width
    inverse_freq = rope_theta ** (-spacing)
    angles = token_places.astype(jnp.float32)[:, None] * inverse_freq[None, :]
    cosine = jnp.cos(angles)[:, None, :]
    sine_part = jnp.sin(angles)[:, None, :]
    front = shaped[:, :, :half_width]
    behind = shaped[:, :, half_width:]
    turned = jnp.concatenate([front * cosine - behind * sine_part, behind * cosine + front * sine_part], axis=2)
    return turned.reshape(row_count, head_count * head_width)

def token_positions(new_labels, old_labels, requests):
    labels = jnp.arange(requests, dtype=jnp.int32)
    member = (new_labels[:, None] == labels[None, :]).astype(jnp.int32)
    cached = lax.optimization_barrier(jnp.sum((old_labels[:, None] == labels[None, :]).astype(jnp.int32), axis=0))
    seg_start = lax.optimization_barrier(jnp.sum((new_labels[:, None] < labels[None, :]).astype(jnp.int32), axis=0))
    offsets = lax.optimization_barrier(jnp.sum(member * (cached - seg_start)[None, :], axis=1))
    return jnp.arange(new_labels.shape[0], dtype=jnp.int32) + offsets

def allowed_keys(new_labels, old_labels):
    row_count = new_labels.shape[0]
    old_part = old_labels[None, :] == new_labels[:, None]
    causal = jnp.arange(row_count)[None, :] <= jnp.arange(row_count)[:, None]
    new_part = (new_labels[None, :] == new_labels[:, None]) & causal
    return jnp.concatenate([old_part, new_part], axis=1)

def attend_head(query_head, key_head, value_head, allowed):
    scores = lax.dot_general(query_head, key_head, (((1,), (1,)), ((), ())), preferred_element_type=jnp.float32)
    scores = jnp.where(allowed, scores * query_head.shape[1] ** (-0.5), -jnp.inf)
    row_max = lax.optimization_barrier(jnp.max(scores, axis=1, keepdims=True))
    weights = jnp.exp(scores - row_max)
    row_total = lax.optimization_barrier(jnp.sum(weights, axis=1, keepdims=True))
    mixed_rows = jnp.dot(weights.astype(jnp.bfloat16), value_head, preferred_element_type=jnp.float32)
    return (mixed_rows / row_total).astype(jnp.bfloat16)

def slot_table(route_block, expert_count, capacity):
    flat_routes = route_block.reshape(-1)
    member = (flat_routes[:, None] == jnp.arange(expert_count, dtype=jnp.int32)[None, :]).astype(jnp.int32)
    before = jnp.cumsum(member, axis=0) - member
    slot_in = lax.optimization_barrier(jnp.sum(before * member, axis=1))
    slot_index = flat_routes * capacity + slot_in
    token_ids = jnp.arange(flat_routes.shape[0], dtype=jnp.int32) // route_block.shape[1]
    holders = jnp.full((expert_count * capacity,), -1, jnp.int32).at[slot_index].set(token_ids)
    return (slot_index, holders)

def reference(tokens, attention_norm_gain, expert_norm_gain, query_projection, key_projection, value_projection, attention_output_weight, cached_keys, cached_values, token_request, cached_request, adapter_of_request, adapter_table_row, adapter_down_maps, adapter_query_up, adapter_value_up, routes, routed_weight, expert_gate_weight, expert_up_weight, expert_down_weight):
    group_results = QUERY_HEADS // KEY_VALUE_HEADS

    def layer_for_group(group_items):
        group_rows, new_labels, old_labels, adapters, old_keys, old_values = group_items
        normed = rms_norm(group_rows, attention_norm_gain)
        table_rows = adapter_table_row[adapters]
        member = (new_labels[:, None] == jnp.arange(GROUP_REQUESTS, dtype=jnp.int32)[None, :]).astype(jnp.float32)
        spread = jnp.repeat(member, ADAPTER_RANK, axis=1)
        down_selected = adapter_down_maps[table_rows].reshape(GROUP_REQUESTS * ADAPTER_RANK, MODEL_WIDTH)
        low_codes = lax.dot_general(normed, down_selected, (((1,), (1,)), ((), ())), preferred_element_type=jnp.float32)
        low_codes = (low_codes * spread).astype(jnp.bfloat16)
        query_up_selected = adapter_query_up[table_rows].reshape(GROUP_REQUESTS * ADAPTER_RANK, QUERY_HEADS * HEAD_SIZE)
        value_up_selected = adapter_value_up[table_rows].reshape(GROUP_REQUESTS * ADAPTER_RANK, KEY_VALUE_HEADS * HEAD_SIZE)
        query_rows = jnp.dot(normed, query_projection, preferred_element_type=jnp.float32) + jnp.dot(low_codes, query_up_selected, preferred_element_type=jnp.float32)
        fresh_keys = jnp.dot(normed, key_projection, preferred_element_type=jnp.float32)
        value_new = (jnp.dot(normed, value_projection, preferred_element_type=jnp.float32) + jnp.dot(low_codes, value_up_selected, preferred_element_type=jnp.float32)).astype(jnp.bfloat16)
        token_places = token_positions(new_labels, old_labels, GROUP_REQUESTS)
        query_rows = apply_rotation(query_rows, token_places, QUERY_HEADS).astype(jnp.bfloat16)
        fresh_keys = apply_rotation(fresh_keys, token_places, KEY_VALUE_HEADS).astype(jnp.bfloat16)
        key_rows = jnp.concatenate([old_keys, fresh_keys], axis=0)
        value_rows = jnp.concatenate([old_values, value_new], axis=0)
        allowed = allowed_keys(new_labels, old_labels)

        def one_head(head_id):
            query_head = lax.dynamic_slice_in_dim(query_rows, head_id * HEAD_SIZE, HEAD_SIZE, 1)
            key_head = lax.dynamic_slice_in_dim(key_rows, head_id // group_results * HEAD_SIZE, HEAD_SIZE, 1)
            value_head = lax.dynamic_slice_in_dim(value_rows, head_id // group_results * HEAD_SIZE, HEAD_SIZE, 1)
            return attend_head(query_head, key_head, value_head, allowed)
        attended = lax.map(one_head, jnp.arange(QUERY_HEADS, dtype=jnp.int32))
        attended = jnp.transpose(attended, (1, 0, 2)).reshape(REQUEST_TOKENS, QUERY_HEADS * HEAD_SIZE)
        attn_out = jnp.dot(attended, attention_output_weight, preferred_element_type=jnp.float32)
        return (group_rows.astype(jnp.float32) + attn_out).astype(jnp.bfloat16)
    residual_stream = lax.map(layer_for_group, (tokens.reshape(N_REQ, REQUEST_TOKENS, MODEL_WIDTH), token_request, cached_request, adapter_of_request, cached_keys.reshape(N_REQ, CONTEXT_TOKENS, KEY_VALUE_HEADS * HEAD_SIZE), cached_values.reshape(N_REQ, CONTEXT_TOKENS, KEY_VALUE_HEADS * HEAD_SIZE))).reshape(TOKEN_TOTAL, MODEL_WIDTH)
    ffn_rows = rms_norm(residual_stream, expert_norm_gain)
    block_count = TOKEN_TOTAL // TOK_DEV
    slot_index, holders = jax.vmap(lambda route_block: slot_table(route_block, EXPERTS, EXP_CAP))(routes.reshape(block_count, TOK_DEV, TOP))
    block_base = (jnp.arange(block_count, dtype=jnp.int32) * TOK_DEV)[:, None]
    holders = jnp.where(holders >= 0, holders + block_base, -1)
    slot_gate = jax.vmap(lambda where_to, gate_rows: jnp.zeros((EXPERTS * EXP_CAP,), jnp.float32).at[where_to].set(gate_rows.reshape(-1)))(slot_index, routed_weight.reshape(block_count, TOK_DEV * TOP))
    holders = jnp.transpose(holders.reshape(block_count, EXPERTS, EXP_CAP), (1, 0, 2)).reshape(EXPERTS, block_count * EXP_CAP)
    slot_gate = jnp.transpose(slot_gate.reshape(block_count, EXPERTS, EXP_CAP), (1, 0, 2)).reshape(EXPERTS, block_count * EXP_CAP)
    quarter = FF_E // N_TP

    def add_expert(moe_total, expert_items):
        holder_row, gate_row, gate_weight, up_weight, down_weight = expert_items
        filled = holder_row >= 0
        picked = jnp.take(ffn_rows, jnp.maximum(holder_row, 0), axis=0)
        picked = jnp.where(filled[:, None], picked, jnp.zeros_like(picked))
        gate_part = jnp.dot(picked, gate_weight, preferred_element_type=jnp.float32)
        up_part = jnp.dot(picked, up_weight, preferred_element_type=jnp.float32)
        hidden = (jax.nn.silu(gate_part) * up_part).astype(jnp.bfloat16)
        pieces = hidden.reshape(-1, N_TP, quarter).astype(jnp.float32)
        down_parts = down_weight.reshape(N_TP, quarter, MODEL_WIDTH).astype(jnp.float32)
        partial_value = jnp.einsum('rqf,qfd->qrd', pieces, down_parts)
        expert_rows = lax.optimization_barrier(jnp.sum(partial_value.astype(jnp.bfloat16).astype(jnp.float32), axis=0))
        weighted = jnp.where(filled[:, None], gate_row[:, None] * expert_rows, jnp.zeros_like(expert_rows))
        return (moe_total.at[jnp.maximum(holder_row, 0)].add(weighted), None)
    moe_start = jnp.zeros((TOKEN_TOTAL, MODEL_WIDTH), jnp.float32)
    moe_total = lax.scan(add_expert, moe_start, (holders, slot_gate, expert_gate_weight, expert_up_weight, expert_down_weight))[0]
    return (residual_stream.astype(jnp.float32) + moe_total).astype(jnp.bfloat16)
```

```python
import functools

import jax
import jax.numpy as jnp
from jax import lax
from jax.experimental import pallas as pl
from jax.experimental.pallas import tpu as pltpu
from jax.sharding import PartitionSpec as P

HEAD_SIZE = 64
EXPERTS = 32
TOP = 8
ADAPTER_RANK = 16
GROUP_REQUESTS = 4
LANES = 128
KEY_BLOCK = 512
QUERY_BLOCK = 128
HIDDEN_SCORE = -1e30
DOWN_COLUMNS = 256
UP_INSIDE = False

norm_eps = 1e-05
rope_theta = 10000.0


def rms_norm(row_block, gain_row):
    values = row_block.astype(jnp.float32)
    inv_rms = lax.rsqrt(jnp.mean(values * values, axis=-1, keepdims=True) + norm_eps)
    return (values * inv_rms * gain_row.astype(jnp.float32)).astype(jnp.bfloat16)


def dot_f32(left, right):
    return jnp.dot(left, right, preferred_element_type=jnp.float32)


def projection_kernel(
    heads, kv_heads, x_ref, gain_ref, wq_ref, wk_ref, wv_ref, down_ref, qup_ref, vup_ref,
    spread_ref, cos_ref, sin_ref, q_ref, k_ref, v_ref
):
    normed = rms_norm(x_ref[...], gain_ref[...])
    low = lax.dot_general(
        normed, down_ref[...], (((1,), (1,)), ((), ())), preferred_element_type=jnp.float32
    )
    low = (low * spread_ref[...]).astype(jnp.bfloat16)
    q = dot_f32(normed, wq_ref[...]) + dot_f32(low, qup_ref[...])
    k = dot_f32(normed, wk_ref[...])
    v_ref[...] = (dot_f32(normed, wv_ref[...]) + dot_f32(low, vup_ref[...])).astype(jnp.bfloat16)
    cosine, sine = cos_ref[...], sin_ref[...]
    lane = lax.broadcasted_iota(jnp.int32, cosine.shape, 1)
    front = lane % HEAD_SIZE < HEAD_SIZE // 2
    upper = lane >= HEAD_SIZE

    def turn(piece):
        partner = jnp.where(
            front,
            pltpu.roll(piece, LANES - HEAD_SIZE // 2, 1),
            pltpu.roll(piece, HEAD_SIZE // 2, 1),
        )
        return piece * cosine + partner * sine

    k_ref[...] = turn(k).astype(jnp.bfloat16)
    per_kv = heads // kv_heads
    for piece_id in range(heads // 2):
        turned = turn(q[:, piece_id * LANES : (piece_id + 1) * LANES]) * HEAD_SIZE ** (-0.5)
        swapped = pltpu.roll(turned, HEAD_SIZE, 1)
        for side in range(2):
            head = 2 * piece_id + side
            kv = head // per_kv
            source = turned if kv == side else swapped
            keep = upper if kv == 1 else jnp.logical_not(upper)
            q_ref[head] = jnp.where(keep, source, 0.0).astype(jnp.bfloat16)


def attention_kernel(
    heads, kv_heads, range_ref, q_ref, ck_ref, cv_ref, nk_ref, nv_ref, bound_ref, wo_ref, out_ref
):
    block = pl.program_id(0)
    rows = q_ref.shape[1]
    queries = q_ref[...].reshape(heads * rows, LANES)
    bounds = jnp.concatenate([bound_ref[...]] * heads, axis=1)
    old_start, old_end, new_start, new_end = (bounds[i : i + 1] for i in range(4))

    def score(keys, first, start, end):
        values = lax.dot_general(
            keys, queries, (((1,), (1,)), ((), ())), preferred_element_type=jnp.float32
        )
        place = lax.broadcasted_iota(jnp.int32, values.shape, 0) + first
        return jnp.where((place >= start) & (place < end), values, HIDDEN_SCORE)

    def gather(weights, values):
        return lax.dot_general(
            values, weights.astype(jnp.bfloat16), (((0,), (0,)), ((), ())),
            preferred_element_type=jnp.float32,
        )

    scores = score(nk_ref[...], 0, new_start, new_end)
    top = jnp.max(scores, axis=0, keepdims=True)
    weights = jnp.exp(scores - top)
    total = jnp.sum(weights, axis=0, keepdims=True)
    mixed = gather(weights, nv_ref[...])

    def step(index, carry):
        top, total, mixed = carry
        first = pl.multiple_of(index * KEY_BLOCK, KEY_BLOCK)
        scores = score(ck_ref[pl.ds(first, KEY_BLOCK), :], first, old_start, old_end)
        new_top = jnp.maximum(top, jnp.max(scores, axis=0, keepdims=True))
        shrink = jnp.exp(top - new_top)
        weights = jnp.exp(scores - new_top)
        total = total * shrink + jnp.sum(weights, axis=0, keepdims=True)
        mixed = mixed * shrink + gather(weights, cv_ref[pl.ds(first, KEY_BLOCK), :])
        return new_top, total, mixed

    top, total, mixed = lax.fori_loop(
        range_ref[0, block], range_ref[1, block], step, (top, total, mixed)
    )
    mixed = mixed / total
    per_kv = heads // kv_heads
    pieces = []
    for piece_id in range(heads // 2):
        halves = []
        for head in (2 * piece_id, 2 * piece_id + 1):
            kv = head // per_kv
            halves.append(
                mixed[kv * HEAD_SIZE : (kv + 1) * HEAD_SIZE, head * rows : (head + 1) * rows]
            )
        pieces.append(jnp.transpose(jnp.concatenate(halves, axis=0)).astype(jnp.bfloat16))
    out_ref[...] = dot_f32(jnp.concatenate(pieces, axis=1), wo_ref[...]).astype(jnp.bfloat16)


MESH = pl.DeviceIdType.MESH


def send_to(source, target, send_sem, recv_sem, axis, device):
    return pltpu.make_async_remote_copy(
        src_ref=source, dst_ref=target, send_sem=send_sem, recv_sem=recv_sem,
        device_id={axis: device}, device_id_type=MESH,
    )


def greet(peers):
    barrier = pltpu.get_barrier_semaphore()
    for axis, device in peers:
        pl.semaphore_signal(barrier, inc=1, device_id={axis: device}, device_id_type=MESH)
    pl.semaphore_wait(barrier, len(peers))


def core_partner(place):
    return place + 1 - 2 * (place % 2)


def token_kernel(tp_count, tokens_ref, group_ref, local_sem, x_send, x_recv):
    here = lax.axis_index("tp")
    beside, across = core_partner(here), (here + 2) % tp_count
    greet([("tp", beside), ("tp", across)])
    to_across = send_to(tokens_ref, group_ref.at[here], x_send.at[0], x_recv.at[0], "tp", across)
    to_across.start()
    to_beside = send_to(tokens_ref, group_ref.at[here], x_send.at[1], x_recv.at[1], "tp", beside)
    to_beside.start()
    own_copy = pltpu.make_async_copy(tokens_ref, group_ref.at[here], local_sem)
    own_copy.start()
    to_across.wait()
    forward = send_to(group_ref.at[across], group_ref.at[across], x_send.at[2], x_recv.at[2], "tp",
                      beside)
    forward.start()
    own_copy.wait()
    to_beside.wait()
    forward.wait()


def opening_kernel(
    req_count, stored, notes_ref, table_ref, all_notes_ref, down_ref, qup_ref, vup_ref,
    noted, chosen, arrived, downs, n_send, n_recv, a_send, a_recv, d_send, d_recv
):
    me, here = lax.axis_index("req"), lax.axis_index("tp")
    beside = core_partner(here)
    greet([("req", (me + step) % req_count) for step in range(1, req_count)] + [("tp", beside)])
    note_copies = []
    for step in range(1, req_count):
        copy = send_to(notes_ref, noted.at[step], n_send.at[step], n_recv.at[step], "req",
                       (me + step) % req_count)
        copy.start()
        note_copies.append(copy)

    rows = GROUP_REQUESTS * ADAPTER_RANK
    depth = stored * ADAPTER_RANK
    lane = lax.broadcasted_iota(jnp.int32, (rows, depth), 1)
    row = lax.broadcasted_iota(jnp.int32, (rows, depth), 0)
    same_rank = lane % ADAPTER_RANK == row % ADAPTER_RANK
    slot = (me * stored + lane // ADAPTER_RANK).astype(jnp.float32)

    def select(notes):
        wanted = notes[2 * TOP :, :depth]
        pick = jnp.where(same_rank & (wanted == slot), 1.0, 0.0).astype(jnp.bfloat16)
        return dot_f32(pick, table_ref[...])

    total = select(notes_ref[...])
    all_notes_ref[me] = notes_ref[: 2 * TOP, :]
    adapter_copies = []
    for step in range(1, req_count):
        note_copies[step - 1].wait()
        notes = noted[step]
        source = (me + req_count - step) % req_count
        all_notes_ref[source] = notes[: 2 * TOP, :]
        chosen[step] = select(notes).astype(jnp.bfloat16)
        copy = send_to(chosen.at[step], arrived.at[step], a_send.at[step], a_recv.at[step], "req",
                       source)
        copy.start()
        adapter_copies.append(copy)
    for step in range(1, req_count):
        adapter_copies[step - 1].wait()
        total = total + arrived[step].astype(jnp.float32)
    total = total.astype(jnp.bfloat16)
    down_width = downs.shape[2]
    query_width = qup_ref.shape[1]
    core = here % 2
    downs[core] = total[:, :down_width]
    copy = send_to(downs.at[core], downs.at[core], d_send, d_recv, "tp", beside)
    copy.start()
    qup_ref[...] = total[:, down_width : down_width + query_width]
    vup_ref[...] = total[:, down_width + query_width :]
    copy.wait()
    down_ref[...] = jnp.concatenate([downs[0], downs[1]], axis=1)


def moe_kernel(
    req_count, tp_count, slots, columns, up_inside, partial_ref, tokens_ref, gain_ref, slot_ref,
    place_ref, weight_ref, gate_ref, gate_far_ref, up_ref, up_far_ref, down_ref, out_ref,
    pair, joined, far, arrived, gates, ups, downs, pick, spread, row_weight, picked, hidden,
    result, beside_in, line_out, line_in,
    p_send, p_recv, local_sem, n_send, n_recv, w_send, w_recv, v_send, v_recv, d_send, d_recv,
    g_send, g_recv, zu_send, zu_recv, zd_send, zd_recv, f_send, f_recv, y_send, y_recv,
    z_send, z_recv
):
    me, here = lax.axis_index("req"), lax.axis_index("tp")
    beside, across = core_partner(here), (here + 2) % tp_count
    partner = core_partner(me)
    line = req_count // 2
    side, spot = me % 2, me // 2
    moe = arrived
    other = 1 - side
    experts, width, quarter = gate_ref.shape
    pieces = width // columns
    own_rows = tokens_ref.shape[0]
    line_rows = line * own_rows
    f32, bf16 = jnp.float32, jnp.bfloat16
    greet(
        [("tp", beside), ("tp", across), ("req", partner)]
        + [("req", (me + 2 * step) % req_count) for step in range(1, line)]
    )
    second = send_to(partial_ref.at[(beside + 2) % tp_count], pair.at[1], p_send.at[1],
                     p_recv.at[1], "tp", beside)
    second.start()
    first = send_to(partial_ref.at[beside], pair.at[0], p_send.at[0], p_recv.at[0], "tp", beside)
    first.start()

    def part(ref, number):
        return ref.at[:, :, pl.ds(number * quarter, quarter)]

    def down_part(number):
        return downs.at[:, pl.ds(number * quarter, quarter), :]

    stays = [(gate_ref, part(gates, 0)), (gate_far_ref, part(gates, 1)), (up_ref, part(ups, 0)),
             (down_ref, down_part(0))]
    goes = [(gate_ref, part(gates, 2)), (gate_far_ref, part(gates, 3)), (up_ref, part(ups, 2)),
            (down_ref, down_part(2))]
    if not up_inside:
        stays.append((up_far_ref, part(ups, 1)))
        goes.append((up_far_ref, part(ups, 3)))
    own_copies = [
        pltpu.make_async_copy(source, target, local_sem.at[i])
        for i, (source, target) in enumerate(stays)
    ]
    near_copies = [
        send_to(source, target, n_send.at[i], n_recv.at[i], "tp", beside)
        for i, (source, target) in enumerate(goes)
    ]

    def up_across(expert):
        return send_to(up_ref.at[expert], ups.at[expert, :, pl.ds(quarter, quarter)],
                       w_send.at[expert], w_recv.at[expert], "tp", across)

    def up_forward(expert):
        return send_to(ups.at[expert, :, pl.ds(quarter, quarter)],
                       ups.at[expert, :, pl.ds(3 * quarter, quarter)],
                       v_send.at[expert], v_recv.at[expert], "tp", beside)

    def band(piece):
        return pl.ds(pl.multiple_of(piece * columns, columns), columns)

    def down_across(piece):
        return send_to(down_ref.at[:, :, band(piece)],
                       downs.at[:, pl.ds(quarter, quarter), band(piece)],
                       d_send.at[piece], d_recv.at[piece], "tp", across)

    def down_forward(piece):
        return send_to(downs.at[:, pl.ds(quarter, quarter), band(piece)],
                       downs.at[:, pl.ds(3 * quarter, quarter), band(piece)],
                       g_send.at[piece], g_recv.at[piece], "tp", beside)

    second.wait()
    joined[...] = (partial_ref[across].astype(f32) + pair[1].astype(f32)).astype(bf16)
    last = send_to(joined, far, p_send.at[2], p_recv.at[2], "tp", across)
    last.start()
    first.wait()
    for copy in near_copies + own_copies:
        copy.start()
    own = partial_ref[here].astype(f32) + pair[0].astype(f32) + tokens_ref[...].astype(f32)
    last.wait()
    if up_inside:
        for expert in range(experts):
            up_across(expert).start()
    for piece in range(pieces):
        down_across(piece).start()
    resid = (own + far[...].astype(f32)).astype(bf16)
    joined[...] = resid
    arrived[side, spot] = rms_norm(resid, gain_ref[...])

    def climb(hop, block):
        return send_to(arrived.at[side, block], arrived.at[side, block], zu_send.at[hop],
                       zu_recv.at[hop], "req", (me + 2) % req_count)

    def descend(hop, block):
        return send_to(arrived.at[side, block], arrived.at[side, block], zd_send.at[hop],
                       zd_recv.at[hop], "req", (me + req_count - 2) % req_count)

    def cross(number, block):
        return send_to(arrived.at[side, block], arrived.at[side, block], f_send.at[number],
                       f_recv.at[number], "req", partner)

    def crossed(number, block):
        return send_to(arrived.at[other, block], arrived.at[other, block], f_send.at[number],
                       f_recv.at[number], "req", partner)

    @pl.when(spot < line - 1)
    def _():
        climb(0, spot).start()

    @pl.when(spot > 0)
    def _():
        descend(0, spot).start()

    cross(0, spot).start()

    def prepare(chunk, carry):
        group = (side + chunk) % 2
        place = place_ref[group]
        lane = lax.broadcasted_iota(jnp.int32, (line_rows, experts * slots), 1)
        hit = lane == place[:, 0:1]
        for expert in range(1, experts):
            hit = hit | (lane == place[:, expert : expert + 1])
        spread[chunk] = jnp.where(hit, 1.0, 0.0).astype(bf16)
        for expert in range(experts):
            chosen = (
                lax.broadcasted_iota(jnp.int32, (slots, line_rows), 0) == slot_ref[expert, group]
            )
            pick[chunk, pl.ds(expert * slots, slots), :] = jnp.where(chosen, 1.0, 0.0).astype(bf16)
            row_weight[expert, chunk] = jnp.sum(
                jnp.where(chosen, weight_ref[expert, group], 0.0), axis=1, keepdims=True
            )
        return carry

    lax.fori_loop(0, 2, prepare, 0)
    forwarded = 0
    for hop in range(line - 1):
        @pl.when(spot - 1 - hop >= 0)
        def _():
            block = spot - 1 - hop
            climb(hop, block).wait_recv()
            if hop + 1 < line - 1:
                @pl.when(spot < line - 1)
                def _():
                    climb(hop + 1, block).start()
            cross(1 + hop, block).start()

        @pl.when(spot + 1 + hop < line)
        def _():
            block = spot + 1 + hop
            descend(hop, block).wait_recv()
            if hop + 1 < line - 1:
                @pl.when(spot > 0)
                def _():
                    descend(hop + 1, block).start()
            cross(line + hop, block).start()

        if up_inside and forwarded < experts:
            up_across(forwarded).wait()
            up_forward(forwarded).start()
            forwarded += 1

    def choose(chunk):
        group = (side + chunk) % 2

        def columns_of(piece, carry):
            rows = arrived[group, :, :, band(piece)].reshape(line_rows, columns)
            values = dot_f32(pick[chunk], rows).astype(bf16)
            for expert in range(experts):
                picked[expert, chunk, :, band(piece)] = values[expert * slots : (expert + 1) * slots]
            return carry

        lax.fori_loop(0, pieces, columns_of, 0)

    choose(0)
    if up_inside:
        for expert in range(forwarded, experts):
            up_across(expert).wait()
            up_forward(expert).start()
    crossed(0, spot).wait_recv()
    for hop in range(line - 1):
        @pl.when(spot - 1 - hop >= 0)
        def _():
            crossed(1 + hop, spot - 1 - hop).wait_recv()

        @pl.when(spot + 1 + hop < line)
        def _():
            crossed(line + hop, spot + 1 + hop).wait_recv()

    choose(1)
    cross(0, spot).wait_send()
    for hop in range(line - 1):
        @pl.when((spot < line - 1) & (spot - hop >= 0))
        def _():
            climb(hop, spot - hop).wait_send()

        @pl.when((spot > 0) & (spot + hop < line))
        def _():
            descend(hop, spot + hop).wait_send()

        @pl.when(spot - 1 - hop >= 0)
        def _():
            cross(1 + hop, spot - 1 - hop).wait_send()

        @pl.when(spot + 1 + hop < line)
        def _():
            cross(line + hop, spot + 1 + hop).wait_send()
    for copy in own_copies:
        copy.wait()
    for copy in near_copies:
        copy.wait()

    def feed(expert, carry):
        if up_inside:
            up_forward(expert).wait()
        rows = picked[expert].reshape(2 * slots, width)
        gate = dot_f32(rows, gates[expert])
        up = dot_f32(rows, ups[expert])
        hidden[expert] = (jax.nn.silu(gate) * up).astype(bf16)
        return carry

    lax.fori_loop(0, experts, feed, 0)

    def to_beside(piece):
        return send_to(moe.at[other, :, :, band(piece)], beside_in.at[:, :, band(piece)],
                       y_send.at[piece], y_recv.at[piece], "req", partner)

    def to_line(piece, step):
        return send_to(line_out.at[(spot + step) % line, :, band(piece)],
                       line_in.at[step, :, band(piece)], z_send.at[piece, step],
                       z_recv.at[piece, step], "req", (me + 2 * step) % req_count)

    def finish(piece):
        to_beside(piece).wait()
        line_out[:, :, band(piece)] = (
            moe[side, :, :, band(piece)].astype(f32) + beside_in[:, :, band(piece)].astype(f32)
        ).astype(bf16)
        for step in range(1, line):
            to_line(piece, step).start()

    def produce(piece, carry):
        down_across(piece).wait()
        down_forward(piece).start()
        down_forward(piece).wait()
        for expert in range(experts):
            values = dot_f32(hidden[expert], downs[expert, :, band(piece)])
            for chunk in range(2):
                result[chunk, pl.ds(expert * slots, slots), :] = (
                    values[chunk * slots : (chunk + 1) * slots] * row_weight[expert, chunk]
                ).astype(bf16)
        for chunk in (1, 0):
            total = dot_f32(spread[chunk], result[chunk]).astype(bf16)
            moe[(side + chunk) % 2, :, :, band(piece)] = total.reshape(line, own_rows, columns)
            if chunk == 1:
                to_beside(piece).start()

        @pl.when(piece > 0)
        def _():
            finish(piece - 1)
        return carry

    lax.fori_loop(0, pieces, produce, 0)
    finish(pieces - 1)

    def close(piece, carry):
        total = (
            joined[:, band(piece)].astype(f32) + moe[side, spot, :, band(piece)].astype(f32)
            + beside_in[spot, :, band(piece)].astype(f32)
        )
        for step in range(1, line):
            to_line(piece, step).wait()
            total = total + line_in[step, :, band(piece)].astype(f32)
        out_ref[:, band(piece)] = total.astype(bf16)
        return carry

    lax.fori_loop(0, pieces, close, 0)


def on_device(
    tokens,
    attention_norm_gain,
    expert_norm_gain,
    query_projection,
    key_projection,
    value_projection,
    attention_output_weight,
    cached_keys,
    cached_values,
    token_request,
    cached_request,
    adapter_of_request,
    adapter_table_row,
    adapter_down_maps,
    adapter_query_up,
    adapter_value_up,
    routes,
    routed_weight,
    expert_gate_weight,
    expert_up_weight,
    expert_down_weight,
):
    tp_count = lax.axis_size("tp")
    tp_place = lax.axis_index("tp")
    req_count = lax.axis_size("req")
    req_place = lax.axis_index("req")
    own_rows, width = tokens.shape
    group_size = own_rows * tp_count
    query_width = query_projection.shape[1]
    kv_width = key_projection.shape[1]
    heads = query_width // HEAD_SIZE
    kv_heads = kv_width // HEAD_SIZE
    low_rows = GROUP_REQUESTS * ADAPTER_RANK
    assert tp_count == 4 and kv_heads == 2 and own_rows == QUERY_BLOCK
    capacity = own_rows * TOP // EXPERTS + 2

    own_routes = lax.dynamic_slice_in_dim(routes, tp_place * own_rows, own_rows, 0)
    own_gates = lax.dynamic_slice_in_dim(routed_weight, tp_place * own_rows, own_rows, 0)
    catalog = jnp.arange(adapter_table_row.shape[0], dtype=jnp.int32)
    table_rows = jnp.sum(
        (adapter_of_request[0][:, None] == catalog[None, :]).astype(jnp.int32)
        * adapter_table_row[None, :],
        axis=1,
    )
    wanted = jnp.broadcast_to(
        jnp.repeat(table_rows, ADAPTER_RANK).astype(jnp.float32)[:, None], (low_rows, LANES)
    )
    notes = jnp.concatenate([own_routes.T.astype(jnp.float32), own_gates.T, wanted], axis=0)

    in_vmem = pl.BlockSpec(memory_space=pltpu.VMEM)
    in_place = pl.BlockSpec(memory_space=pl.ANY)
    dma = pltpu.SemaphoreType.DMA
    bf16 = jnp.bfloat16
    group_x = pl.pallas_call(
        functools.partial(token_kernel, tp_count),
        in_specs=[in_vmem],
        out_specs=in_place,
        out_shape=jax.ShapeDtypeStruct((tp_count, own_rows, width), bf16),
        scratch_shapes=[dma, dma((3,)), dma((3,))],
        compiler_params=pltpu.CompilerParams(
            collective_id=4, has_side_effects=True, vmem_limit_bytes=8 << 20
        ),
        cost_estimate=pl.CostEstimate(flops=0, bytes_accessed=40_000_000, transcendentals=0),
        name="tokens",
    )(tokens)
    group_x, expert_gate_weight, expert_up_weight = lax.optimization_barrier(
        (group_x, expert_gate_weight, expert_up_weight)
    )

    across = [(i, i ^ 2) for i in range(tp_count)]

    gate_far, up_far = (
        lax.ppermute(piece, "tp", across) for piece in (expert_gate_weight, expert_up_weight)
    )

    stored = adapter_down_maps.shape[0]
    down_width = width // 2
    down_part = lax.dynamic_slice_in_dim(
        adapter_down_maps, tp_place % 2 * down_width, down_width, 2
    )
    table = jnp.concatenate([down_part, adapter_query_up, adapter_value_up], axis=2)
    adapter_width = table.shape[2]
    table = table.reshape(stored * ADAPTER_RANK, adapter_width)
    notes, group_x = lax.optimization_barrier((notes, group_x))
    notes, down_selected, query_up_selected, value_up_selected = pl.pallas_call(
        functools.partial(opening_kernel, req_count, stored),
        in_specs=[in_vmem] * 2,
        out_specs=[in_vmem] * 4,
        out_shape=[
            jax.ShapeDtypeStruct((req_count, 2 * TOP, own_rows), jnp.float32),
            jax.ShapeDtypeStruct((low_rows, width), bf16),
            jax.ShapeDtypeStruct((low_rows, query_width), bf16),
            jax.ShapeDtypeStruct((low_rows, kv_width), bf16),
        ],
        scratch_shapes=[
            pltpu.VMEM((req_count,) + notes.shape, jnp.float32),
            pltpu.VMEM((req_count, low_rows, adapter_width), bf16),
            pltpu.VMEM((req_count, low_rows, adapter_width), bf16),
            pltpu.VMEM((2, low_rows, down_width), bf16),
            dma((req_count,)), dma((req_count,)), dma((req_count,)), dma((req_count,)), dma, dma,
        ],
        compiler_params=pltpu.CompilerParams(
            collective_id=1, has_side_effects=True, vmem_limit_bytes=32 << 20
        ),
        cost_estimate=pl.CostEstimate(flops=0, bytes_accessed=90_000_000, transcendentals=0),
        name="opening",
    )(notes, table)
    group_x = group_x.reshape(group_size, width)
    all_routes = notes[:, :TOP].astype(jnp.int32)
    all_gates = notes[:, TOP:]

    new_labels = token_request[0]
    old_labels = cached_request[0]
    labels = jnp.arange(GROUP_REQUESTS, dtype=jnp.int32)
    member = new_labels[:, None] == labels[None, :]
    old_below = jnp.sum((old_labels[:, None] < labels[None, :]).astype(jnp.int32), axis=0)
    old_upto = jnp.sum((old_labels[:, None] <= labels[None, :]).astype(jnp.int32), axis=0)
    new_below = jnp.sum((new_labels[:, None] < labels[None, :]).astype(jnp.int32), axis=0)

    def by_token(table):
        return jnp.sum(jnp.where(member, table[None, :], 0), axis=1)

    place = jnp.arange(group_size, dtype=jnp.int32)
    old_start, old_end, new_start = by_token(old_below), by_token(old_upto), by_token(new_below)
    positions = place - new_start + old_end - old_start
    bounds = jnp.stack([old_start, old_end, new_start, place + 1] * 2, axis=0)
    block_start = jnp.min(old_start.reshape(-1, QUERY_BLOCK), axis=1)
    block_end = jnp.max(old_end.reshape(-1, QUERY_BLOCK), axis=1)
    block_range = jnp.stack(
        [block_start // KEY_BLOCK, (block_end + KEY_BLOCK - 1) // KEY_BLOCK], axis=0
    )
    spread = jnp.repeat(member.astype(jnp.float32), ADAPTER_RANK, axis=1)
    half = HEAD_SIZE // 2
    lane = jnp.arange(LANES, dtype=jnp.int32)
    inverse_freq = rope_theta ** (-((lane % half).astype(jnp.float32) / half))
    angles = positions.astype(jnp.float32)[:, None] * inverse_freq[None, :]
    cosine = jnp.cos(angles)
    sine = jnp.sin(angles) * jnp.where(lane % HEAD_SIZE < half, -1.0, 1.0)[None, :]

    whole = lambda shape: pl.BlockSpec(shape, lambda i, *_: (0,) * len(shape))
    by_row = lambda rows, columns: pl.BlockSpec((rows, columns), lambda i, *_: (i, 0))
    rows = 2 * QUERY_BLOCK
    queries, fresh_keys, fresh_values = pl.pallas_call(
        functools.partial(projection_kernel, heads, kv_heads),
        grid=(group_size // rows,),
        in_specs=[
            by_row(rows, width), whole((1, width)), whole((width, query_width)),
            whole((width, kv_width)), whole((width, kv_width)), whole((low_rows, width)),
            whole((low_rows, query_width)), whole((low_rows, kv_width)), by_row(rows, low_rows),
            by_row(rows, LANES), by_row(rows, LANES),
        ],
        out_specs=[
            pl.BlockSpec((heads, rows, LANES), lambda i: (0, i, 0)),
            by_row(rows, kv_width), by_row(rows, kv_width),
        ],
        out_shape=[
            jax.ShapeDtypeStruct((heads, group_size, LANES), jnp.bfloat16),
            jax.ShapeDtypeStruct((group_size, kv_width), jnp.bfloat16),
            jax.ShapeDtypeStruct((group_size, kv_width), jnp.bfloat16),
        ],
        cost_estimate=pl.CostEstimate(
            flops=2 * group_size * width * (query_width + 2 * kv_width + low_rows),
            bytes_accessed=6_000_000, transcendentals=0,
        ),
        name="projections",
    )(
        group_x, attention_norm_gain[None, :], query_projection, key_projection, value_projection,
        down_selected, query_up_selected, value_up_selected, spread, cosine, sine,
    )

    context = cached_keys.shape[0]
    partial_rows = pl.pallas_call(
        functools.partial(attention_kernel, heads, kv_heads),
        grid_spec=pltpu.PrefetchScalarGridSpec(
            num_scalar_prefetch=1,
            grid=(group_size // QUERY_BLOCK,),
            in_specs=[
                pl.BlockSpec((heads, QUERY_BLOCK, LANES), lambda i, *_: (0, i, 0)),
                whole((context, kv_width)), whole((context, kv_width)),
                whole((group_size, kv_width)), whole((group_size, kv_width)),
                pl.BlockSpec((8, QUERY_BLOCK), lambda i, *_: (0, i)),
                whole((query_width, width)),
            ],
            out_specs=by_row(QUERY_BLOCK, width),
        ),
        out_shape=jax.ShapeDtypeStruct((group_size, width), jnp.bfloat16),
        compiler_params=pltpu.CompilerParams(vmem_limit_bytes=40 << 20),
        cost_estimate=pl.CostEstimate(
            flops=10_000_000_000, bytes_accessed=6_000_000, transcendentals=14_000_000
        ),
        name="attention",
    )(
        block_range, queries, cached_keys, cached_values, fresh_keys, fresh_values, bounds,
        attention_output_weight,
    )
    local_experts, _, quarter = expert_gate_weight.shape
    line = req_count // 2
    line_rows = line * own_rows
    slots = -(-line * capacity // 16) * 16
    expert_ids = req_place * local_experts + jnp.arange(local_experts, dtype=jnp.int32)
    hits = all_routes[None] == expert_ids[:, None, None, None]
    expert_weight = jnp.sum(jnp.where(hits, all_gates[None], 0.0), axis=2)
    named = jnp.any(hits, axis=2)
    earlier = jnp.arange(own_rows)[:, None] < jnp.arange(own_rows)[None, :]
    rank = jnp.einsum(
        "ebt,tu->ebu", named.astype(jnp.bfloat16), earlier.astype(jnp.bfloat16),
        preferred_element_type=jnp.float32,
    ).astype(jnp.int32)
    block_base = (jnp.arange(req_count, dtype=jnp.int32) // 2) * capacity

    def by_side(values):
        values = values.reshape(local_experts, line, 2, own_rows)
        return values.transpose(0, 2, 1, 3).reshape(local_experts, 2, line_rows)

    slot_of = by_side(jnp.where(named, rank + block_base[None, :, None], -1))
    expert_weight = by_side(expert_weight)[:, :, None, :]
    expert_base = jnp.arange(local_experts, dtype=jnp.int32) * slots
    place_of = jnp.where(slot_of >= 0, slot_of + expert_base[:, None, None], -1)
    place_of = place_of.transpose(1, 2, 0)
    slot_of = slot_of[:, :, None, :]

    pieces = width // DOWN_COLUMNS
    stays = 4 if UP_INSIDE else 5
    vmem = pltpu.VMEM
    block = (own_rows, width)
    full = 4 * quarter
    return pl.pallas_call(
        functools.partial(moe_kernel, req_count, tp_count, slots, DOWN_COLUMNS, UP_INSIDE),
        in_specs=[in_vmem] * 6 + [in_place] * 5,
        out_specs=in_vmem,
        out_shape=jax.ShapeDtypeStruct(block, bf16),
        scratch_shapes=[
            vmem((2,) + block, bf16), vmem(block, bf16), vmem(block, bf16),
            vmem((2, line) + block, bf16),
            vmem((local_experts, width, full), bf16), vmem((local_experts, width, full), bf16),
            vmem((local_experts, full, width), bf16),
            vmem((2, local_experts * slots, line_rows), bf16),
            vmem((2, line_rows, local_experts * slots), bf16),
            vmem((local_experts, 2, slots, 1), jnp.float32),
            vmem((local_experts, 2, slots, width), bf16),
            vmem((local_experts, 2 * slots, full), bf16),
            vmem((2, local_experts * slots, DOWN_COLUMNS), bf16),
            vmem((line,) + block, bf16), vmem((line,) + block, bf16),
            vmem((line,) + block, bf16),
            dma((3,)), dma((3,)), dma((stays,)), dma((stays,)), dma((stays,)),
            dma((local_experts,)), dma((local_experts,)), dma((local_experts,)),
            dma((local_experts,)), dma((pieces,)), dma((pieces,)), dma((pieces,)), dma((pieces,)),
            dma((line - 1,)), dma((line - 1,)), dma((line - 1,)), dma((line - 1,)),
            dma((2 * line - 1,)), dma((2 * line - 1,)), dma((pieces,)), dma((pieces,)),
            dma((pieces, line)), dma((pieces, line)),
        ],
        compiler_params=pltpu.CompilerParams(
            collective_id=2, has_side_effects=True, vmem_limit_bytes=60 << 20
        ),
        cost_estimate=pl.CostEstimate(
            flops=0, bytes_accessed=300_000_000, transcendentals=0
        ),
        name="moe",
    )(
        partial_rows.reshape(tp_count, own_rows, width), tokens, expert_norm_gain[None, :],
        slot_of, place_of, expert_weight, expert_gate_weight, gate_far, expert_up_weight, up_far,
        expert_down_weight,
    )


def solution(mesh):
    return jax.shard_map(
        on_device,
        mesh=mesh,
        in_specs=(
            P(("req", "tp"), None),
            P(),
            P(),
            P(None, "tp"),
            P(None, "tp"),
            P(None, "tp"),
            P("tp", None),
            P("req", "tp"),
            P("req", "tp"),
            P("req", None),
            P("req", None),
            P("req", None),
            P(),
            P("req", None, None),
            P("req", None, "tp"),
            P("req", None, "tp"),
            P("req", None),
            P("req", None),
            P("req", None, "tp"),
            P("req", None, "tp"),
            P("req", "tp", None),
        ),
        out_specs=P(("req", "tp"), None),
        check_vma=False,
    )
```

```python
import functools

import jax
import jax.numpy as jnp
import numpy as np
from jax import lax
from jax.experimental import pallas as pl
from jax.experimental.pallas import tpu as pltpu
from jax.sharding import PartitionSpec as P

HEAD_SIZE = 64
EXPERTS = 32
TOP = 8
ADAPTER_RANK = 16
GROUP_REQUESTS = 4
LANES = 128
KEY_BLOCK = 512
QUERY_BLOCK = 128
HIDDEN_SCORE = -1e30
DOWN_COLUMNS = 256

norm_eps = 1e-05
rope_theta = 10000.0


def rms_norm(row_block, gain_row):
    values = row_block.astype(jnp.float32)
    inv_rms = lax.rsqrt(jnp.mean(values * values, axis=-1, keepdims=True) + norm_eps)
    return (values * inv_rms * gain_row).astype(jnp.bfloat16)


def dot_f32(left, right):
    return jnp.dot(left, right, preferred_element_type=jnp.float32)


def attention_kernel(
    heads, kv_heads, range_ref, q_ref, ck_ref, cv_ref, nk_ref, nv_ref, bound_ref, wo_ref, out_ref
):
    block = pl.program_id(0)
    rows = q_ref.shape[1]
    queries = q_ref[...].reshape(heads * rows, LANES)
    bounds = jnp.concatenate([bound_ref[...]] * heads, axis=1)
    old_start, old_end, new_start, new_end = (bounds[i : i + 1] for i in range(4))

    def score(keys, first, start, end):
        values = lax.dot_general(
            keys, queries, (((1,), (1,)), ((), ())), preferred_element_type=jnp.float32
        )
        place = lax.broadcasted_iota(jnp.int32, values.shape, 0) + first
        return jnp.where((place >= start) & (place < end), values, HIDDEN_SCORE)

    def gather(weights, values):
        return lax.dot_general(
            values, weights.astype(jnp.bfloat16), (((0,), (0,)), ((), ())),
            preferred_element_type=jnp.float32,
        )

    scores = score(nk_ref[...], 0, new_start, new_end)
    top = jnp.max(scores, axis=0, keepdims=True)
    weights = jnp.exp(scores - top)
    total = jnp.sum(weights, axis=0, keepdims=True)
    mixed = gather(weights, nv_ref[...])

    def step(index, carry):
        top, total, mixed = carry
        first = pl.multiple_of(index * KEY_BLOCK, KEY_BLOCK)
        scores = score(ck_ref[pl.ds(first, KEY_BLOCK), :], first, old_start, old_end)
        new_top = jnp.maximum(top, jnp.max(scores, axis=0, keepdims=True))
        shrink = jnp.exp(top - new_top)
        weights = jnp.exp(scores - new_top)
        total = total * shrink + jnp.sum(weights, axis=0, keepdims=True)
        mixed = mixed * shrink + gather(weights, cv_ref[pl.ds(first, KEY_BLOCK), :])
        return new_top, total, mixed

    top, total, mixed = lax.fori_loop(
        range_ref[0, block], range_ref[1, block], step, (top, total, mixed)
    )
    mixed = mixed / total
    per_kv = heads // kv_heads
    pieces = []
    for piece_id in range(heads // 2):
        halves = []
        for head in (2 * piece_id, 2 * piece_id + 1):
            kv = head // per_kv
            halves.append(
                mixed[kv * HEAD_SIZE : (kv + 1) * HEAD_SIZE, head * rows : (head + 1) * rows]
            )
        pieces.append(jnp.transpose(jnp.concatenate(halves, axis=0)).astype(jnp.bfloat16))
    out_ref[...] = dot_f32(jnp.concatenate(pieces, axis=1), wo_ref[...]).astype(jnp.bfloat16)


MESH = pl.DeviceIdType.MESH


def send_to(source, target, send_sem, recv_sem, axis, device):
    return pltpu.make_async_remote_copy(
        src_ref=source, dst_ref=target, send_sem=send_sem, recv_sem=recv_sem,
        device_id={axis: device}, device_id_type=MESH,
    )


def greet(peers):
    barrier = pltpu.get_barrier_semaphore()
    for axis, device in peers:
        pl.semaphore_signal(barrier, inc=1, device_id={axis: device}, device_id_type=MESH)
    pl.semaphore_wait(barrier, len(peers))


def weight_plan(experts):
    head = min(2, experts)
    rest = min(3, experts - 1)
    return head, rest, 2 * experts - head - rest


def core_partner(place):
    return place + 1 - 2 * (place % 2)


def opening_kernel(
    req_count, tp_count, heads, kv_heads, tokens_ref, gain_ref, wq_ref, wk_ref, wv_ref,
    request_ref, cached_ref, adapter_ref, row_ref, down_ref, qup_ref, vup_ref, routes_ref,
    routed_ref, freq_ref, gate_ref, up_ref, q_ref, k_ref, v_ref, notes_ref, bounds_ref,
    head_ref, rest_ref,
    group, normed, weights, table, q_part, v_part, cosines, sines, note, noted, near_out,
    near_in, line_out, line_in, downs, qups, vups, bounce,
    local_sem, x_send, x_recv, n_send, n_recv, y_send, y_recv, z_send, z_recv, d_send, d_recv,
    w_send, w_recv, bounce_sem
):
    me, here = lax.axis_index("req"), lax.axis_index("tp")
    beside, across = core_partner(here), (here + 2) % tp_count
    partner = core_partner(me)
    line = req_count // 2
    side, spot = me % 2, me // 2
    other = 1 - side
    f32, bf16 = jnp.float32, jnp.bfloat16
    corner = core_partner(across)
    own_rows, width = tokens_ref.shape
    stored = down_ref.shape[0]
    query_width, kv_width = wq_ref.shape[1], wk_ref.shape[1]
    part = width // tp_count
    edges = (0, part, part + query_width, part + query_width + kv_width)

    own_down = down_ref.at[:, :, pl.ds(pl.multiple_of(here * part, part), part)]
    pieces = [
        (tokens_ref, group.at[here]),
        (own_down, table.at[:, :, edges[0] : edges[1]]),
        (qup_ref, table.at[:, :, edges[1] : edges[2]]),
        (vup_ref, table.at[:, :, edges[2] : edges[3]]),
        (wq_ref, weights.at[:, 0:query_width]),
        (wk_ref, weights.at[:, query_width : query_width + kv_width]),
        (wv_ref, weights.at[:, query_width + kv_width :]),
    ]
    local = [
        pltpu.make_async_copy(source, target, local_sem.at[i])
        for i, (source, target) in enumerate(pieces)
    ]
    experts, depth_all, quarter = gate_ref.shape
    head, rest, _ = weight_plan(experts)
    sources = [gate_ref.at[i] for i in range(experts)] + [up_ref.at[i] for i in range(experts)]
    rest_copies = [
        pltpu.make_async_copy(sources[head + i], bounce.at[i], bounce_sem.at[i])
        for i in range(rest)
    ]
    bounce_copy = pltpu.make_async_copy(bounce, rest_ref, bounce_sem.at[rest])
    half_rows = depth_all // 2
    head_copies = [
        send_to(gate_ref.at[i // 2, pl.ds(i % 2 * half_rows, half_rows)],
                head_ref.at[i // 2, pl.ds(i % 2 * half_rows, half_rows)],
                w_send.at[i], w_recv.at[i], "tp", across)
        for i in range(2 * head)
    ]
    for copy in local + rest_copies:
        copy.start()
    greet(
        [("req", (me + step) % req_count) for step in range(1, req_count)]
        + [("tp", beside), ("tp", across), ("tp", corner)]
    )
    to_across = send_to(tokens_ref, group.at[here], x_send.at[0], x_recv.at[0], "tp", across)
    to_across.start()
    for copy in head_copies[:3]:
        copy.start()

    rows_here = pl.ds(pl.multiple_of(here * own_rows, own_rows), own_rows)
    note[:TOP, :] = routes_ref[:, rows_here].astype(f32)
    note[TOP : 2 * TOP, :] = routed_ref[:, rows_here]
    wanted = [
        jnp.full((1, LANES), row_ref[adapter_ref[0, i]], jnp.int32) for i in range(GROUP_REQUESTS)
    ]
    note[2 * TOP :, :] = jnp.concatenate(wanted + wanted, axis=0).astype(f32)

    def tell(step):
        return send_to(note, noted.at[me], n_send.at[step], n_recv.at[me], "req",
                       (me + step) % req_count)

    def told(source):
        return send_to(note, noted.at[source], n_send.at[0], n_recv.at[source], "req", partner)

    for step in range(1, req_count):
        tell(step).start()
    to_beside = send_to(tokens_ref, group.at[here], x_send.at[1], x_recv.at[1], "tp", beside)
    to_beside.start()
    noted[me] = note[...]

    labels = request_ref[...]
    old_labels = cached_ref[...]

    def count(mask):
        return jnp.sum(jnp.where(mask, 1.0, 0.0), axis=1, keepdims=True).astype(jnp.int32)

    new_below = [count(labels < i) for i in range(GROUP_REQUESTS)]
    old_below = [count(old_labels < i) for i in range(GROUP_REQUESTS + 1)]
    zero = jnp.zeros_like(labels)
    new_start, old_start, old_end = zero, zero, zero
    for i in range(GROUP_REQUESTS):
        member = labels == i
        new_start = jnp.where(member, new_below[i], new_start)
        old_start = jnp.where(member, old_below[i], old_start)
        old_end = jnp.where(member, old_below[i + 1], old_end)
    next_place = lax.broadcasted_iota(jnp.int32, labels.shape, 1) + 1
    bounds_ref[...] = jnp.concatenate([old_start, old_end, new_start, next_place] * 2, axis=0)
    place = lax.broadcasted_iota(jnp.int32, (tp_count * own_rows, LANES), 0)
    moved = jnp.zeros_like(place)
    for i in range(GROUP_REQUESTS):
        offset = old_below[i + 1] - old_below[i] - new_below[i]
        moved = jnp.where(place >= new_below[i], offset, moved)
    lane = lax.broadcasted_iota(jnp.int32, (2 * own_rows, LANES), 1)
    front = lane % HEAD_SIZE < HEAD_SIZE // 2
    upper = lane >= HEAD_SIZE
    low_rows = GROUP_REQUESTS * ADAPTER_RANK
    depth = stored * ADAPTER_RANK
    column = lax.broadcasted_iota(jnp.int32, (low_rows, depth), 1)
    row = lax.broadcasted_iota(jnp.int32, (low_rows, depth), 0)
    same_rank = column % ADAPTER_RANK == row % ADAPTER_RANK
    slot = (me * stored + column // ADAPTER_RANK).astype(f32)

    def select(source):
        rows = [
            jnp.broadcast_to(noted[source, pl.ds(2 * TOP + i, 1), :], (ADAPTER_RANK, LANES))
            for i in range(GROUP_REQUESTS)
        ]
        sought = jnp.concatenate(rows, axis=0)[:, :depth]
        pick = jnp.where(same_rank & (sought == slot), 1.0, 0.0).astype(bf16)
        return dot_f32(pick, table[...].reshape(depth, edges[3]))

    def to_near(goal):
        return send_to(near_out.at[goal], near_in.at[goal], y_send.at[goal], y_recv.at[goal],
                       "req", partner)

    def to_line(step):
        return send_to(line_out.at[step], line_in.at[step], z_send.at[step], z_recv.at[step],
                       "req", (me + 2 * step) % req_count)

    for copy in local[1:4]:
        copy.wait()
    for step in list(range(1, line)) + [0]:
        goal = (spot + step) % line
        told(2 * goal + other).wait_recv()
        near_out[goal] = select(2 * goal + other).astype(bf16)
        to_near(goal).start()

    angles = (place + moved).astype(f32) * freq_ref[...]
    cosines[...] = jnp.cos(angles)
    sines[...] = jnp.sin(angles)

    def turn(piece, rows):
        rolled = jnp.where(
            front,
            -pltpu.roll(piece, LANES - HEAD_SIZE // 2, 1),
            pltpu.roll(piece, HEAD_SIZE // 2, 1),
        )
        return piece * cosines[rows, :] + rolled * sines[rows, :]

    def rows_of(pair):
        return pl.ds(pl.multiple_of(pair * 2 * own_rows, 2 * own_rows), 2 * own_rows)

    def project(pair):
        rows = rows_of(pair)
        values = rms_norm(group[pl.ds(2 * pair, 2)].reshape(2 * own_rows, width), gain_ref[0:1, :])
        normed[rows, :] = values
        product = dot_f32(values, weights[...])
        q_part[rows, :] = product[:, :query_width]
        k_ref[rows, :] = turn(product[:, query_width : query_width + kv_width], rows).astype(bf16)
        v_part[rows, :] = product[:, query_width + kv_width :]

    own_pair = here // 2
    for copy in rest_copies:
        copy.wait()
    bounce_copy.start()
    local[0].wait()
    for copy in local[4:]:
        copy.wait()
    to_beside.wait()
    forward = send_to(group.at[across], group.at[across], x_send.at[2], x_recv.at[2], "tp", beside)
    for step in range(1, line):
        goal = (spot + step) % line
        to_near(goal).wait_recv()
        told(2 * goal + side).wait_recv()
        line_out[step] = (select(2 * goal + side) + near_in[goal].astype(f32)).astype(bf16)
        to_line(step).start()
        if step == 1:
            project(own_pair)
        if step == min(2, line - 1):
            to_across.wait()
            forward.start()
    forward.wait()
    project(1 - own_pair)
    to_near(spot).wait_recv()
    for source in range(req_count):
        notes_ref[source] = noted[source, : 2 * TOP, :]
    total = select(me) + near_in[spot].astype(f32)
    for step in range(1, line):
        to_line(step).wait_recv()
        total = total + line_in[step].astype(f32)
    total = total.astype(bf16)

    def down_columns(owner):
        return downs.at[:, pl.ds(pl.multiple_of(owner * part, part), part)]

    downs[:, pl.ds(pl.multiple_of(here * part, part), part)] = total[:, edges[0] : edges[1]]
    down_copies = [
        send_to(down_columns(here), down_columns(here), d_send.at[i], d_recv.at[i], "tp", device)
        for i, device in enumerate((across, corner, beside))
    ]
    for copy in down_copies + head_copies[3:]:
        copy.start()
    qups[...] = total[:, edges[1] : edges[2]]
    vups[...] = total[:, edges[2] : edges[3]]
    for copy in down_copies:
        copy.wait()
    per_kv = heads // kv_heads

    def complete(pair, carry):
        rows = rows_of(pair)
        low = lax.dot_general(
            downs[...], normed[rows, :], (((1,), (1,)), ((), ())), preferred_element_type=f32
        )
        owner = lax.broadcasted_iota(jnp.int32, low.shape, 0) // ADAPTER_RANK
        low = jnp.where(owner == request_ref[:, rows], low, 0.0).astype(bf16)

        def raised(ups):
            return lax.dot_general(
                low, ups, (((0,), (0,)), ((), ())), preferred_element_type=f32
            )

        v_ref[rows, :] = (v_part[rows, :] + raised(vups[...])).astype(bf16)
        q = q_part[rows, :] + raised(qups[...])
        for piece_id in range(heads // 2):
            turned = turn(q[:, piece_id * LANES : (piece_id + 1) * LANES], rows)
            turned = turned * HEAD_SIZE ** (-0.5)
            swapped = pltpu.roll(turned, HEAD_SIZE, 1)
            for half in range(2):
                head = 2 * piece_id + half
                kv = head // per_kv
                source = turned if kv == half else swapped
                keep = upper if kv == 1 else jnp.logical_not(upper)
                q_ref[head, rows, :] = jnp.where(keep, source, 0.0).astype(bf16)
        return carry

    lax.fori_loop(0, 2, complete, 0)
    for copy in head_copies:
        copy.wait()
    bounce_copy.wait()
    for step in range(1, req_count):
        tell(step).wait_send()
    for step in range(line):
        to_near((spot + step) % line).wait_send()
    for step in range(1, line):
        to_line(step).wait_send()


def moe_kernel(
    req_count, tp_count, slots, columns, partial_ref, tokens_ref, gain_ref, slot_ref,
    place_ref, weight_ref, gate_ref, gate_head_ref, up_ref, weight_rest_ref, down_ref,
    out_ref,
    pair, joined, far, arrived, gates, ups, downs, pick, spread, row_weight, picked, hidden,
    result, beside_in, line_out, line_in,
    p_send, p_recv, local_sem, n_send, n_recv, w_send, w_recv, v_send, v_recv, d_send, d_recv,
    g_send, g_recv, zu_send, zu_recv, zd_send, zd_recv, f_send, f_recv, y_send, y_recv,
    z_send, z_recv
):
    me, here = lax.axis_index("req"), lax.axis_index("tp")
    beside, across = core_partner(here), (here + 2) % tp_count
    partner = core_partner(me)
    line = req_count // 2
    side, spot = me % 2, me // 2
    moe = arrived
    other = 1 - side
    experts, width, quarter = gate_ref.shape
    pieces = width // columns
    own_rows = tokens_ref.shape[0]
    line_rows = line * own_rows
    f32, bf16 = jnp.float32, jnp.bfloat16
    greet(
        [("tp", beside), ("tp", across), ("req", partner)]
        + [("req", (me + 2 * step) % req_count) for step in range(1, line)]
    )
    second = send_to(partial_ref.at[(beside + 2) % tp_count], pair.at[1], p_send.at[1],
                     p_recv.at[1], "tp", beside)
    second.start()
    first = send_to(partial_ref.at[beside], pair.at[0], p_send.at[0], p_recv.at[0], "tp", beside)
    first.start()

    def part(ref, number, first=0, count=experts):
        return ref.at[first : first + count, :, pl.ds(number * quarter, quarter)]

    def down_part(number):
        return downs.at[:, pl.ds(number * quarter, quarter), :]

    head, rest, inside = weight_plan(experts)
    held = [(gate_ref, gates, 0, 0, experts), (up_ref, ups, 0, 0, experts),
            (gate_head_ref, gates, 1, 0, head)]
    if experts > head:
        held.append((weight_rest_ref.at[: experts - head], gates, 1, head, experts - head))
    if experts > inside:
        held.append((weight_rest_ref.at[experts - head : rest], ups, 1, 0, experts - inside))
    stays = [(ref, part(target, *where)) for ref, target, *where in held]
    goes = [(ref, part(target, number + 2, *where)) for ref, target, number, *where in held]
    stays.append((down_ref, down_part(0)))
    goes.append((down_ref, down_part(2)))
    own_copies = [
        pltpu.make_async_copy(source, target, local_sem.at[i])
        for i, (source, target) in enumerate(stays)
    ]
    near_copies = [
        send_to(source, target, n_send.at[i], n_recv.at[i], "tp", beside)
        for i, (source, target) in enumerate(goes)
    ]

    first_late = experts - inside

    def late_part(place, number):
        return ups.at[first_late + place, :, pl.ds(number * quarter, quarter)]

    late_across = [
        send_to(up_ref.at[first_late + i], late_part(i, 1), w_send.at[i], w_recv.at[i], "tp", across)
        for i in range(inside)
    ]
    late_forward = [
        send_to(late_part(i, 1), late_part(i, 3), v_send.at[i], v_recv.at[i], "tp", beside)
        for i in range(inside)
    ]

    def band(piece):
        return pl.ds(pl.multiple_of(piece * columns, columns), columns)

    def down_across(piece):
        return send_to(down_ref.at[:, :, band(piece)],
                       downs.at[:, pl.ds(quarter, quarter), band(piece)],
                       d_send.at[piece], d_recv.at[piece], "tp", across)

    def down_forward(piece):
        return send_to(downs.at[:, pl.ds(quarter, quarter), band(piece)],
                       downs.at[:, pl.ds(3 * quarter, quarter), band(piece)],
                       g_send.at[piece], g_recv.at[piece], "tp", beside)

    second.wait()
    joined[...] = (partial_ref[across].astype(f32) + pair[1].astype(f32)).astype(bf16)
    last = send_to(joined, far, p_send.at[2], p_recv.at[2], "tp", across)
    last.start()
    first.wait()
    for copy in near_copies + own_copies:
        copy.start()
    own = partial_ref[here].astype(f32) + pair[0].astype(f32) + tokens_ref[...].astype(f32)
    last.wait()
    for copy in late_across:
        copy.start()
    for piece in range(pieces):
        down_across(piece).start()
    resid = (own + far[...].astype(f32)).astype(bf16)
    joined[...] = resid
    arrived[side, spot] = rms_norm(resid, gain_ref[1:2, :])

    def climb(hop, block):
        return send_to(arrived.at[side, block], arrived.at[side, block], zu_send.at[hop],
                       zu_recv.at[hop], "req", (me + 2) % req_count)

    def descend(hop, block):
        return send_to(arrived.at[side, block], arrived.at[side, block], zd_send.at[hop],
                       zd_recv.at[hop], "req", (me + req_count - 2) % req_count)

    def cross(number, block):
        return send_to(arrived.at[side, block], arrived.at[side, block], f_send.at[number],
                       f_recv.at[number], "req", partner)

    def crossed(number, block):
        return send_to(arrived.at[other, block], arrived.at[other, block], f_send.at[number],
                       f_recv.at[number], "req", partner)

    @pl.when(spot < line - 1)
    def _():
        climb(0, spot).start()

    @pl.when(spot > 0)
    def _():
        descend(0, spot).start()

    cross(0, spot).start()

    def prepare(chunk, carry):
        group = (side + chunk) % 2
        place = place_ref[group]
        lane = lax.broadcasted_iota(jnp.int32, (line_rows, experts * slots), 1)
        hit = lane == place[:, 0:1]
        for expert in range(1, experts):
            hit = hit | (lane == place[:, expert : expert + 1])
        spread[chunk] = jnp.where(hit, 1.0, 0.0).astype(bf16)
        for expert in range(experts):
            chosen = (
                lax.broadcasted_iota(jnp.int32, (slots, line_rows), 0) == slot_ref[expert, group]
            )
            pick[chunk, pl.ds(expert * slots, slots), :] = jnp.where(chosen, 1.0, 0.0).astype(bf16)
            row_weight[expert, chunk] = jnp.sum(
                jnp.where(chosen, weight_ref[expert, group], 0.0), axis=1, keepdims=True
            )
        return carry

    lax.fori_loop(0, 2, prepare, 0)
    forwarded = 0
    for hop in range(line - 1):
        @pl.when(spot - 1 - hop >= 0)
        def _():
            block = spot - 1 - hop
            climb(hop, block).wait_recv()
            if hop + 1 < line - 1:
                @pl.when(spot < line - 1)
                def _():
                    climb(hop + 1, block).start()
            cross(1 + hop, block).start()

        @pl.when(spot + 1 + hop < line)
        def _():
            block = spot + 1 + hop
            descend(hop, block).wait_recv()
            if hop + 1 < line - 1:
                @pl.when(spot > 0)
                def _():
                    descend(hop + 1, block).start()
            cross(line + hop, block).start()

        if forwarded < inside:
            late_across[forwarded].wait()
            late_forward[forwarded].start()
            forwarded += 1

    def choose(chunk):
        group = (side + chunk) % 2

        def columns_of(piece, carry):
            rows = arrived[group, :, :, band(piece)].reshape(line_rows, columns)
            values = dot_f32(pick[chunk], rows).astype(bf16)
            for expert in range(experts):
                picked[expert, chunk, :, band(piece)] = values[expert * slots : (expert + 1) * slots]
            return carry

        lax.fori_loop(0, pieces, columns_of, 0)

    def feed(chunk):
        def expert_of(expert, carry):
            rows = picked[expert, chunk]
            gate = dot_f32(rows, gates[expert])
            up = dot_f32(rows, ups[expert])
            hidden[expert, pl.ds(chunk * slots, slots), :] = (jax.nn.silu(gate) * up).astype(bf16)
            return carry

        lax.fori_loop(0, experts, expert_of, 0)

    choose(0)
    for expert in range(forwarded, inside):
        late_across[expert].wait()
        late_forward[expert].start()
    for copy in own_copies + near_copies + late_forward:
        copy.wait()
    feed(0)
    crossed(0, spot).wait_recv()
    for hop in range(line - 1):
        @pl.when(spot - 1 - hop >= 0)
        def _():
            crossed(1 + hop, spot - 1 - hop).wait_recv()

        @pl.when(spot + 1 + hop < line)
        def _():
            crossed(line + hop, spot + 1 + hop).wait_recv()

    choose(1)
    feed(1)
    cross(0, spot).wait_send()
    for hop in range(line - 1):
        @pl.when((spot < line - 1) & (spot - hop >= 0))
        def _():
            climb(hop, spot - hop).wait_send()

        @pl.when((spot > 0) & (spot + hop < line))
        def _():
            descend(hop, spot + hop).wait_send()

        @pl.when(spot - 1 - hop >= 0)
        def _():
            cross(1 + hop, spot - 1 - hop).wait_send()

        @pl.when(spot + 1 + hop < line)
        def _():
            cross(line + hop, spot + 1 + hop).wait_send()

    def to_beside(piece):
        return send_to(moe.at[other, :, :, band(piece)], beside_in.at[:, :, band(piece)],
                       y_send.at[piece], y_recv.at[piece], "req", partner)

    def to_line(piece, step):
        return send_to(line_out.at[(spot + step) % line, :, band(piece)],
                       line_in.at[step, :, band(piece)], z_send.at[piece, step],
                       z_recv.at[piece, step], "req", (me + 2 * step) % req_count)

    def finish(piece):
        to_beside(piece).wait()
        line_out[:, :, band(piece)] = (
            moe[side, :, :, band(piece)].astype(f32) + beside_in[:, :, band(piece)].astype(f32)
        ).astype(bf16)
        for step in range(1, line):
            to_line(piece, step).start()

    def produce(piece, carry):
        down_across(piece).wait()
        down_forward(piece).start()
        down_forward(piece).wait()
        for expert in range(experts):
            values = dot_f32(hidden[expert], downs[expert, :, band(piece)])
            for chunk in range(2):
                result[chunk, pl.ds(expert * slots, slots), :] = (
                    values[chunk * slots : (chunk + 1) * slots] * row_weight[expert, chunk]
                ).astype(bf16)
        for chunk in (1, 0):
            total = dot_f32(spread[chunk], result[chunk]).astype(bf16)
            moe[(side + chunk) % 2, :, :, band(piece)] = total.reshape(line, own_rows, columns)
            if chunk == 1:
                to_beside(piece).start()

        @pl.when(piece > 0)
        def _():
            finish(piece - 1)
        return carry

    lax.fori_loop(0, pieces, produce, 0)
    finish(pieces - 1)

    def close(piece, carry):
        total = (
            joined[:, band(piece)].astype(f32) + moe[side, spot, :, band(piece)].astype(f32)
            + beside_in[spot, :, band(piece)].astype(f32)
        )
        for step in range(1, line):
            to_line(piece, step).wait()
            total = total + line_in[step, :, band(piece)].astype(f32)
        out_ref[:, band(piece)] = total.astype(bf16)
        return carry

    lax.fori_loop(0, pieces, close, 0)


def on_device(
    tokens,
    attention_norm_gain,
    expert_norm_gain,
    query_projection,
    key_projection,
    value_projection,
    attention_output_weight,
    cached_keys,
    cached_values,
    token_request,
    cached_request,
    adapter_of_request,
    adapter_table_row,
    adapter_down_maps,
    adapter_query_up,
    adapter_value_up,
    routes,
    routed_weight,
    expert_gate_weight,
    expert_up_weight,
    expert_down_weight,
):
    tp_count = lax.axis_size("tp")
    req_count = lax.axis_size("req")
    req_place = lax.axis_index("req")
    own_rows, width = tokens.shape
    group_size = own_rows * tp_count
    query_width = query_projection.shape[1]
    kv_width = key_projection.shape[1]
    heads = query_width // HEAD_SIZE
    kv_heads = kv_width // HEAD_SIZE
    low_rows = GROUP_REQUESTS * ADAPTER_RANK
    assert tp_count == 4 and kv_heads == 2 and own_rows == QUERY_BLOCK
    capacity = own_rows * TOP // EXPERTS + 2

    in_vmem = pl.BlockSpec(memory_space=pltpu.VMEM)
    in_place = pl.BlockSpec(memory_space=pl.ANY)
    dma = pltpu.SemaphoreType.DMA
    bf16 = jnp.bfloat16
    line = req_count // 2
    part = width // tp_count
    adapter_width = part + query_width + kv_width
    in_smem = pl.BlockSpec(memory_space=pltpu.SMEM)
    vmem = pltpu.VMEM
    f32 = jnp.float32
    half = HEAD_SIZE // 2
    inverse_freq = jnp.asarray(rope_theta ** (-(np.arange(LANES) % half) / half), f32)
    gains = jnp.stack([attention_norm_gain, expert_norm_gain]).astype(f32)
    adapter_block = (line, low_rows, adapter_width)
    head, rest, inside = weight_plan(expert_gate_weight.shape[0])
    head_shape = jax.ShapeDtypeStruct((head,) + expert_gate_weight.shape[1:], bf16)
    rest_shape = jax.ShapeDtypeStruct((max(rest, 1),) + expert_gate_weight.shape[1:], bf16)
    queries, fresh_keys, fresh_values, notes, bounds, gate_head, weight_rest = pl.pallas_call(
        functools.partial(opening_kernel, req_count, tp_count, heads, kv_heads),
        in_specs=[in_place, in_vmem, in_place, in_place, in_place, in_vmem, in_vmem, in_smem,
                  in_smem, in_place, in_place, in_place, in_vmem, in_vmem, in_vmem, in_place, in_place],
        out_specs=[in_vmem] * 5 + [in_place] * 2,
        out_shape=[
            jax.ShapeDtypeStruct((heads, group_size, LANES), bf16),
            jax.ShapeDtypeStruct((group_size, kv_width), bf16),
            jax.ShapeDtypeStruct((group_size, kv_width), bf16),
            jax.ShapeDtypeStruct((req_count, 2 * TOP, own_rows), f32),
            jax.ShapeDtypeStruct((8, group_size), jnp.int32),
            head_shape, rest_shape,
        ],
        scratch_shapes=[
            vmem((tp_count, own_rows, width), bf16), vmem((group_size, width), bf16),
            vmem((width, query_width + 2 * kv_width), bf16),
            vmem((adapter_down_maps.shape[0], ADAPTER_RANK, adapter_width), bf16),
            vmem((group_size, query_width), f32), vmem((group_size, kv_width), f32),
            vmem((group_size, LANES), f32), vmem((group_size, LANES), f32),
            vmem((3 * TOP, LANES), f32), vmem((req_count, 3 * TOP, LANES), f32),
            vmem(adapter_block, bf16), vmem(adapter_block, bf16), vmem(adapter_block, bf16),
            vmem(adapter_block, bf16), vmem((low_rows, width), bf16),
            vmem((low_rows, query_width), bf16), vmem((low_rows, kv_width), bf16),
            vmem(rest_shape.shape, bf16),
            dma((7,)), dma((3,)), dma((3,)), dma((req_count,)), dma((req_count,)), dma((line,)),
            dma((line,)), dma((line,)), dma((line,)), dma((3,)), dma((3,)),
            dma((2 * head,)), dma((2 * head,)), dma((rest + 1,)),
        ],
        compiler_params=pltpu.CompilerParams(
            collective_id=1, has_side_effects=True, vmem_limit_bytes=60 << 20
        ),
        cost_estimate=pl.CostEstimate(flops=0, bytes_accessed=300_000_000, transcendentals=0),
        name="opening",
    )(
        tokens, gains, query_projection, key_projection, value_projection,
        token_request, cached_request, adapter_of_request, adapter_table_row, adapter_down_maps,
        adapter_query_up, adapter_value_up, routes.T, routed_weight.T, inverse_freq[None, :],
        expert_gate_weight, expert_up_weight,
    )
    if rest:
        weight_rest = lax.ppermute(weight_rest, "tp", [(i, i ^ 2) for i in range(tp_count)])
    all_routes = notes[:, :TOP].astype(jnp.int32)
    all_gates = notes[:, TOP:]

    old_start, old_end = bounds[0], bounds[1]
    block_start = jnp.min(old_start.reshape(-1, QUERY_BLOCK), axis=1)
    block_end = jnp.max(old_end.reshape(-1, QUERY_BLOCK), axis=1)
    block_range = jnp.stack(
        [block_start // KEY_BLOCK, (block_end + KEY_BLOCK - 1) // KEY_BLOCK], axis=0
    )
    whole = lambda shape: pl.BlockSpec(shape, lambda i, *_: (0,) * len(shape))
    by_row = lambda rows, columns: pl.BlockSpec((rows, columns), lambda i, *_: (i, 0))
    context = cached_keys.shape[0]
    partial_rows = pl.pallas_call(
        functools.partial(attention_kernel, heads, kv_heads),
        grid_spec=pltpu.PrefetchScalarGridSpec(
            num_scalar_prefetch=1,
            grid=(group_size // QUERY_BLOCK,),
            in_specs=[
                pl.BlockSpec((heads, QUERY_BLOCK, LANES), lambda i, *_: (0, i, 0)),
                whole((context, kv_width)), whole((context, kv_width)),
                whole((group_size, kv_width)), whole((group_size, kv_width)),
                pl.BlockSpec((8, QUERY_BLOCK), lambda i, *_: (0, i)),
                whole((query_width, width)),
            ],
            out_specs=by_row(QUERY_BLOCK, width),
        ),
        out_shape=jax.ShapeDtypeStruct((group_size, width), jnp.bfloat16),
        compiler_params=pltpu.CompilerParams(vmem_limit_bytes=56 << 20),
        cost_estimate=pl.CostEstimate(
            flops=0, bytes_accessed=1_000_000, transcendentals=0
        ),
        name="attention",
    )(
        block_range, queries, cached_keys, cached_values, fresh_keys, fresh_values, bounds,
        attention_output_weight,
    )
    local_experts, _, quarter = expert_gate_weight.shape
    line_rows = line * own_rows
    slots = -(-line * capacity // 16) * 16
    expert_ids = req_place * local_experts + jnp.arange(local_experts, dtype=jnp.int32)
    hits = all_routes[None] == expert_ids[:, None, None, None]
    expert_weight = jnp.sum(jnp.where(hits, all_gates[None], 0.0), axis=2)
    named = jnp.any(hits, axis=2)
    earlier = jnp.arange(own_rows)[:, None] < jnp.arange(own_rows)[None, :]
    rank = jnp.einsum(
        "ebt,tu->ebu", named.astype(jnp.bfloat16), earlier.astype(jnp.bfloat16),
        preferred_element_type=jnp.float32,
    ).astype(jnp.int32)
    block_base = (jnp.arange(req_count, dtype=jnp.int32) // 2) * capacity

    def by_side(values):
        values = values.reshape(local_experts, line, 2, own_rows)
        return values.transpose(0, 2, 1, 3).reshape(local_experts, 2, line_rows)

    slot_of = by_side(jnp.where(named, rank + block_base[None, :, None], -1))
    expert_weight = by_side(expert_weight)[:, :, None, :]
    expert_base = jnp.arange(local_experts, dtype=jnp.int32) * slots
    place_of = jnp.where(slot_of >= 0, slot_of + expert_base[:, None, None], -1)
    place_of = place_of.transpose(1, 2, 0)
    slot_of = slot_of[:, :, None, :]

    pieces = width // DOWN_COLUMNS
    held = 4 + (local_experts > head) + (local_experts > inside)
    block = (own_rows, width)
    full = 4 * quarter
    return pl.pallas_call(
        functools.partial(moe_kernel, req_count, tp_count, slots, DOWN_COLUMNS),
        in_specs=[in_vmem] * 6 + [in_place] * 5,
        out_specs=in_vmem,
        out_shape=jax.ShapeDtypeStruct(block, bf16),
        scratch_shapes=[
            vmem((2,) + block, bf16), vmem(block, bf16), vmem(block, bf16),
            vmem((2, line) + block, bf16),
            vmem((local_experts, width, full), bf16), vmem((local_experts, width, full), bf16),
            vmem((local_experts, full, width), bf16),
            vmem((2, local_experts * slots, line_rows), bf16),
            vmem((2, line_rows, local_experts * slots), bf16),
            vmem((local_experts, 2, slots, 1), jnp.float32),
            vmem((local_experts, 2, slots, width), bf16),
            vmem((local_experts, 2 * slots, full), bf16),
            vmem((2, local_experts * slots, DOWN_COLUMNS), bf16),
            vmem((line,) + block, bf16), vmem((line,) + block, bf16),
            vmem((line,) + block, bf16),
            dma((3,)), dma((3,)), dma((held,)), dma((held,)), dma((held,)),
            dma((inside,)), dma((inside,)), dma((inside,)), dma((inside,)),
            dma((pieces,)), dma((pieces,)), dma((pieces,)), dma((pieces,)),
            dma((line - 1,)), dma((line - 1,)), dma((line - 1,)), dma((line - 1,)),
            dma((2 * line - 1,)), dma((2 * line - 1,)), dma((pieces,)), dma((pieces,)),
            dma((pieces, line)), dma((pieces, line)),
        ],
        compiler_params=pltpu.CompilerParams(
            collective_id=2, has_side_effects=True, vmem_limit_bytes=60 << 20
        ),
        cost_estimate=pl.CostEstimate(
            flops=0, bytes_accessed=300_000_000, transcendentals=0
        ),
        name="moe",
    )(
        partial_rows.reshape(tp_count, own_rows, width), tokens, gains,
        slot_of, place_of, expert_weight, expert_gate_weight, gate_head, expert_up_weight, weight_rest,
        expert_down_weight,
    )


def solution(mesh):
    return jax.shard_map(
        on_device,
        mesh=mesh,
        in_specs=(
            P(("req", "tp"), None),
            P(),
            P(),
            P(None, "tp"),
            P(None, "tp"),
            P(None, "tp"),
            P("tp", None),
            P("req", "tp"),
            P("req", "tp"),
            P("req", None),
            P("req", None),
            P("req", None),
            P(),
            P("req", None, None),
            P("req", None, "tp"),
            P("req", None, "tp"),
            P("req", None),
            P("req", None),
            P("req", None, "tp"),
            P("req", None, "tp"),
            P("req", "tp", None),
        ),
        out_specs=P(("req", "tp"), None),
        check_vma=False,
    )
```

```python
import functools

import jax
import jax.numpy as jnp
import numpy as np
from jax import lax
from jax.experimental import pallas as pl
from jax.experimental.pallas import tpu as pltpu
from jax.sharding import PartitionSpec as P

HEAD_SIZE = 64
EXPERTS = 32
TOP = 8
ADAPTER_RANK = 16
GROUP_REQUESTS = 4
LANES = 128
KEY_BLOCK = 512
QUERY_BLOCK = 128
HIDDEN_SCORE = -1e30
LOG2_E = 1.4426950408889634
DOWN_COLUMNS = 128
PICK_COLUMNS = 256
CROSS_ROWS = 48

norm_eps = 1e-05
rope_theta = 10000.0


def rms_norm(row_block, gain_row):
    values = row_block.astype(jnp.float32)
    inv_rms = lax.rsqrt(jnp.mean(values * values, axis=-1, keepdims=True) + norm_eps)
    return (values * inv_rms * gain_row).astype(jnp.bfloat16)


def dot_f32(left, right):
    return jnp.dot(left, right, preferred_element_type=jnp.float32)


def attention_kernel(
    heads, kv_heads, range_ref, q_ref, bias_ref, edge_ref, ck_ref, cv_ref, nk_ref, nv_ref, wo_ref,
    out_ref
):
    block = pl.program_id(0)
    rows = q_ref.shape[1]
    queries = jnp.concatenate(
        [q_ref[...].reshape(heads * rows, LANES), jnp.concatenate([bias_ref[...]] * heads, axis=0)],
        axis=1,
    )

    def score(keys, first, edge):
        place = lax.broadcasted_iota(jnp.int32, (keys.shape[0], LANES), 0) + first
        inside = (place >= edge_ref[edge : edge + 1, :]) & (place < edge_ref[edge + 1 : edge + 2, :])
        marks = jnp.where(inside, 1.0, 0.0).astype(jnp.bfloat16)
        return lax.dot_general(
            jnp.concatenate([keys, marks], axis=1), queries, (((1,), (1,)), ((), ())),
            preferred_element_type=jnp.float32,
        )

    def gather(weights, values):
        return lax.dot_general(
            values, weights.astype(jnp.bfloat16), (((0,), (0,)), ((), ())),
            preferred_element_type=jnp.float32,
        )

    def step(keys_ref, values_ref, size, edge, index, carry):
        top, total, mixed = carry
        first = pl.multiple_of(index * size, size)
        scores = score(keys_ref[pl.ds(first, size), :], first, edge)
        new_top = jnp.maximum(top, jnp.max(scores, axis=0, keepdims=True))
        shrink = jnp.exp2(top - new_top)
        weights = jnp.exp2(scores - new_top)
        total = total * shrink + jnp.sum(weights, axis=0, keepdims=True)
        mixed = mixed * shrink + gather(weights, values_ref[pl.ds(first, size), :])
        return new_top, total, mixed

    first = pl.multiple_of(block * rows, rows)
    scores = score(nk_ref[pl.ds(first, rows), :], first, 2)
    key_row = lax.broadcasted_iota(jnp.int32, scores.shape, 0)
    query_row = lax.broadcasted_iota(jnp.int32, scores.shape, 1) % rows
    scores = jnp.where(key_row <= query_row, scores, HIDDEN_SCORE)
    top = jnp.max(scores, axis=0, keepdims=True)
    weights = jnp.exp2(scores - top)
    total = jnp.sum(weights, axis=0, keepdims=True)
    mixed = gather(weights, nv_ref[pl.ds(first, rows), :])
    carry = lax.fori_loop(
        0, block, functools.partial(step, nk_ref, nv_ref, rows, 2), (top, total, mixed)
    )
    top, total, mixed = lax.fori_loop(
        range_ref[0, block], range_ref[1, block],
        functools.partial(step, ck_ref, cv_ref, KEY_BLOCK, 0), carry
    )
    mixed = mixed / total
    per_kv = heads // kv_heads
    pieces = []
    for piece_id in range(heads // 2):
        halves = []
        for head in (2 * piece_id, 2 * piece_id + 1):
            kv = head // per_kv
            halves.append(
                mixed[kv * HEAD_SIZE : (kv + 1) * HEAD_SIZE, head * rows : (head + 1) * rows]
            )
        pieces.append(jnp.transpose(jnp.concatenate(halves, axis=0)).astype(jnp.bfloat16))
    out_ref[...] = dot_f32(jnp.concatenate(pieces, axis=1), wo_ref[...]).astype(jnp.bfloat16)


MESH = pl.DeviceIdType.MESH


def send_to(source, target, send_sem, recv_sem, axis, device):
    return pltpu.make_async_remote_copy(
        src_ref=source, dst_ref=target, send_sem=send_sem, recv_sem=recv_sem,
        device_id={axis: device}, device_id_type=MESH,
    )


def greet(peers):
    barrier = pltpu.get_barrier_semaphore()
    for axis, device in peers:
        pl.semaphore_signal(barrier, inc=1, device_id={axis: device}, device_id_type=MESH)
    pl.semaphore_wait(barrier, len(peers))


def weight_plan(experts):
    head = 1
    rest = min(3, experts - 1)
    return head, rest, 2 * experts - head - rest


def core_partner(place):
    return place + 1 - 2 * (place % 2)


def opening_kernel(
    req_count, tp_count, heads, kv_heads, tokens_ref, gain_ref, wq_ref, wk_ref, wv_ref,
    request_ref, cached_ref, adapter_ref, row_ref, down_ref, qup_ref, vup_ref, routes_ref,
    routed_ref, freq_ref, gate_ref, up_ref, q_ref, k_ref, v_ref, notes_ref, range_ref,
    edge_ref, bias_ref, head_ref, rest_ref,
    group, normed, weights, table, q_part, v_part, cosines, sines, note, noted, near_out,
    near_in, line_out, line_in, downs, qups, vups, bounce,
    local_sem, x_send, x_recv, n_send, n_recv, y_send, y_recv, z_send, z_recv, d_send, d_recv,
    w_send, w_recv, bounce_sem
):
    me, here = lax.axis_index("req"), lax.axis_index("tp")
    beside, across = core_partner(here), (here + 2) % tp_count
    partner = core_partner(me)
    line = req_count // 2
    side, spot = me % 2, me // 2
    other = 1 - side
    f32, bf16 = jnp.float32, jnp.bfloat16
    corner = core_partner(across)
    own_rows, width = tokens_ref.shape
    stored = down_ref.shape[0]
    query_width, kv_width = wq_ref.shape[1], wk_ref.shape[1]
    part = width // tp_count
    edges = (0, part, part + query_width, part + query_width + kv_width)

    own_down = down_ref.at[:, :, pl.ds(pl.multiple_of(here * part, part), part)]
    pieces = [
        (tokens_ref, group.at[here]),
        (own_down, table.at[:, :, edges[0] : edges[1]]),
        (qup_ref, table.at[:, :, edges[1] : edges[2]]),
        (vup_ref, table.at[:, :, edges[2] : edges[3]]),
        (wq_ref, weights.at[:, 0:query_width]),
        (wk_ref, weights.at[:, query_width : query_width + kv_width]),
        (wv_ref, weights.at[:, query_width + kv_width :]),
    ]
    local = [
        pltpu.make_async_copy(source, target, local_sem.at[i])
        for i, (source, target) in enumerate(pieces)
    ]
    experts, depth_all, quarter = gate_ref.shape
    head, rest, _ = weight_plan(experts)
    sources = [gate_ref.at[i] for i in range(experts)] + [up_ref.at[i] for i in range(experts)]
    rest_copies = [
        pltpu.make_async_copy(sources[head + i], bounce.at[i], bounce_sem.at[i])
        for i in range(rest)
    ]
    bounce_copy = pltpu.make_async_copy(bounce, rest_ref, bounce_sem.at[rest])
    half_rows = depth_all // 2
    head_copies = [
        send_to(gate_ref.at[i // 2, pl.ds(i % 2 * half_rows, half_rows)],
                head_ref.at[i // 2, pl.ds(i % 2 * half_rows, half_rows)],
                w_send.at[i], w_recv.at[i], "tp", across)
        for i in range(2 * head)
    ]
    for copy in local + rest_copies:
        copy.start()
    greet(
        [("req", (me + step) % req_count) for step in range(1, req_count)]
        + [("tp", beside), ("tp", across), ("tp", corner)]
    )
    to_across = send_to(tokens_ref, group.at[here], x_send.at[0], x_recv.at[0], "tp", across)
    to_across.start()
    for copy in head_copies[:3]:
        copy.start()

    rows_here = pl.ds(pl.multiple_of(here * own_rows, own_rows), own_rows)
    note[:TOP, :] = routes_ref[:, rows_here].astype(f32)
    note[TOP : 2 * TOP, :] = routed_ref[:, rows_here]
    wanted = [
        jnp.full((1, LANES), row_ref[adapter_ref[0, i]], jnp.int32) for i in range(GROUP_REQUESTS)
    ]
    note[2 * TOP :, :] = jnp.concatenate(wanted + wanted, axis=0).astype(f32)

    def tell(step):
        return send_to(note, noted.at[me], n_send.at[step], n_recv.at[me], "req",
                       (me + step) % req_count)

    def told(source):
        return send_to(note, noted.at[source], n_send.at[0], n_recv.at[source], "req", partner)

    for step in range(1, req_count):
        tell(step).start()
    to_beside = send_to(tokens_ref, group.at[here], x_send.at[1], x_recv.at[1], "tp", beside)
    to_beside.start()
    noted[me] = note[...]

    labels = request_ref[...]
    old_labels = cached_ref[...]

    def count(mask):
        return jnp.sum(jnp.where(mask, 1.0, 0.0), axis=1, keepdims=True).astype(jnp.int32)

    new_below = [count(labels < i) for i in range(GROUP_REQUESTS)]
    old_below = [count(old_labels < i) for i in range(GROUP_REQUESTS + 1)]
    new_below.append(count(labels < GROUP_REQUESTS))
    column = lax.broadcasted_iota(jnp.int32, (1, LANES), 1)
    edges_of = []
    for below in (old_below, new_below):
        low_edge = jnp.zeros_like(column)
        high_edge = jnp.zeros_like(column)
        for i in range(GROUP_REQUESTS):
            low_edge = jnp.where(column == i, below[i], low_edge)
            high_edge = jnp.where(column == i, below[i + 1], high_edge)
        edges_of += [low_edge, high_edge]
    edge_ref[...] = jnp.concatenate(edges_of * 2, axis=0)
    old_start, old_end = jnp.zeros_like(labels), jnp.zeros_like(labels)
    for i in range(GROUP_REQUESTS):
        member = labels == i
        old_start = jnp.where(member, old_below[i], old_start)
        old_end = jnp.where(member, old_below[i + 1], old_end)
    starts, ends = jnp.zeros_like(column), jnp.zeros_like(column)
    for i in range(tp_count):
        block = slice(i * own_rows, (i + 1) * own_rows)
        start = jnp.min(old_start[:, block].astype(f32), axis=1, keepdims=True).astype(jnp.int32)
        end = jnp.max(old_end[:, block].astype(f32), axis=1, keepdims=True).astype(jnp.int32)
        starts = jnp.where(column == i, start // KEY_BLOCK, starts)
        ends = jnp.where(column == i, (end + KEY_BLOCK - 1) // KEY_BLOCK, ends)
    range_ref[...] = jnp.concatenate([starts, ends] * 4, axis=0)
    place = lax.broadcasted_iota(jnp.int32, (tp_count * own_rows, LANES), 0)
    moved = jnp.zeros_like(place)
    request = jnp.zeros_like(place)
    for i in range(GROUP_REQUESTS):
        offset = old_below[i + 1] - old_below[i] - new_below[i]
        moved = jnp.where(place >= new_below[i], offset, moved)
        request = jnp.where(place >= new_below[i], i, request)
    label = lax.broadcasted_iota(jnp.int32, place.shape, 1)
    hidden_pair = (label < GROUP_REQUESTS) & (label != request)
    bias_ref[...] = jnp.where(hidden_pair, HIDDEN_SCORE, 0.0).astype(bf16)
    lane = lax.broadcasted_iota(jnp.int32, (2 * own_rows, LANES), 1)
    front = lane % HEAD_SIZE < HEAD_SIZE // 2
    upper = lane >= HEAD_SIZE
    low_rows = GROUP_REQUESTS * ADAPTER_RANK
    depth = stored * ADAPTER_RANK
    column = lax.broadcasted_iota(jnp.int32, (low_rows, depth), 1)
    row = lax.broadcasted_iota(jnp.int32, (low_rows, depth), 0)
    same_rank = column % ADAPTER_RANK == row % ADAPTER_RANK
    slot = (me * stored + column // ADAPTER_RANK).astype(f32)

    def select(source):
        rows = [
            jnp.broadcast_to(noted[source, pl.ds(2 * TOP + i, 1), :], (ADAPTER_RANK, LANES))
            for i in range(GROUP_REQUESTS)
        ]
        sought = jnp.concatenate(rows, axis=0)[:, :depth]
        pick = jnp.where(same_rank & (sought == slot), 1.0, 0.0).astype(bf16)
        return dot_f32(pick, table[...].reshape(depth, edges[3]))

    def to_near(goal):
        return send_to(near_out.at[goal], near_in.at[goal], y_send.at[goal], y_recv.at[goal],
                       "req", partner)

    def to_line(step):
        return send_to(line_out.at[step], line_in.at[step], z_send.at[step], z_recv.at[step],
                       "req", (me + 2 * step) % req_count)

    for copy in local[1:4]:
        copy.wait()
    for step in list(range(1, line)) + [0]:
        goal = (spot + step) % line
        told(2 * goal + other).wait_recv()
        near_out[goal] = select(2 * goal + other).astype(bf16)
        to_near(goal).start()

    angles = (place + moved).astype(f32) * freq_ref[...]
    cosines[...] = jnp.cos(angles)
    sines[...] = jnp.sin(angles)

    def turn(piece, rows):
        rolled = jnp.where(
            front,
            -pltpu.roll(piece, LANES - HEAD_SIZE // 2, 1),
            pltpu.roll(piece, HEAD_SIZE // 2, 1),
        )
        return piece * cosines[rows, :] + rolled * sines[rows, :]

    def rows_of(pair):
        return pl.ds(pl.multiple_of(pair * 2 * own_rows, 2 * own_rows), 2 * own_rows)

    def project(pair):
        rows = rows_of(pair)
        values = rms_norm(group[pl.ds(2 * pair, 2)].reshape(2 * own_rows, width), gain_ref[0:1, :])
        normed[rows, :] = values
        product = dot_f32(values, weights[...])
        q_part[rows, :] = product[:, :query_width]
        k_ref[rows, :] = turn(product[:, query_width : query_width + kv_width], rows).astype(bf16)
        v_part[rows, :] = product[:, query_width + kv_width :]

    own_pair = here // 2
    for copy in rest_copies:
        copy.wait()
    bounce_copy.start()
    local[0].wait()
    for copy in local[4:]:
        copy.wait()
    to_beside.wait()
    forward = send_to(group.at[across], group.at[across], x_send.at[2], x_recv.at[2], "tp", beside)
    for step in range(1, line):
        goal = (spot + step) % line
        to_near(goal).wait_recv()
        told(2 * goal + side).wait_recv()
        line_out[step] = (select(2 * goal + side) + near_in[goal].astype(f32)).astype(bf16)
        to_line(step).start()
        if step == 1:
            project(own_pair)
        if step == min(2, line - 1):
            to_across.wait()
            forward.start()
    forward.wait()
    project(1 - own_pair)
    to_near(spot).wait_recv()
    for source in range(req_count):
        notes_ref[source] = noted[source, : 2 * TOP, :]
    total = select(me) + near_in[spot].astype(f32)
    for step in range(1, line):
        to_line(step).wait_recv()
        total = total + line_in[step].astype(f32)
    total = total.astype(bf16)

    def down_columns(owner):
        return downs.at[:, pl.ds(pl.multiple_of(owner * part, part), part)]

    downs[:, pl.ds(pl.multiple_of(here * part, part), part)] = total[:, edges[0] : edges[1]]
    down_copies = [
        send_to(down_columns(here), down_columns(here), d_send.at[i], d_recv.at[i], "tp", device)
        for i, device in enumerate((across, corner, beside))
    ]
    for copy in down_copies + head_copies[3:]:
        copy.start()
    qups[...] = total[:, edges[1] : edges[2]]
    vups[...] = total[:, edges[2] : edges[3]]
    for copy in down_copies:
        copy.wait()
    per_kv = heads // kv_heads

    def complete(pair, carry):
        rows = rows_of(pair)
        low = lax.dot_general(
            downs[...], normed[rows, :], (((1,), (1,)), ((), ())), preferred_element_type=f32
        )
        owner = lax.broadcasted_iota(jnp.int32, low.shape, 0) // ADAPTER_RANK
        low = jnp.where(owner == request_ref[:, rows], low, 0.0).astype(bf16)

        def raised(ups):
            return lax.dot_general(
                low, ups, (((0,), (0,)), ((), ())), preferred_element_type=f32
            )

        v_ref[rows, :] = (v_part[rows, :] + raised(vups[...])).astype(bf16)
        q = q_part[rows, :] + raised(qups[...])
        for piece_id in range(heads // 2):
            turned = turn(q[:, piece_id * LANES : (piece_id + 1) * LANES], rows)
            turned = turned * (HEAD_SIZE ** (-0.5) * LOG2_E)
            swapped = pltpu.roll(turned, HEAD_SIZE, 1)
            for half in range(2):
                head = 2 * piece_id + half
                kv = head // per_kv
                source = turned if kv == half else swapped
                keep = upper if kv == 1 else jnp.logical_not(upper)
                q_ref[head, rows, :] = jnp.where(keep, source, 0.0).astype(bf16)
        return carry

    lax.fori_loop(0, 2, complete, 0)
    for copy in head_copies:
        copy.wait()
    bounce_copy.wait()
    for step in range(1, req_count):
        tell(step).wait_send()
    for step in range(line):
        to_near((spot + step) % line).wait_send()
    for step in range(1, line):
        to_line(step).wait_send()


def moe_kernel(
    req_count, tp_count, slots, columns, partial_ref, tokens_ref, gain_ref, slot_ref,
    place_ref, weight_ref, gate_ref, gate_head_ref, up_ref, weight_rest_ref, down_ref,
    out_ref,
    pair, joined, far, arrived, gates, ups, downs, pick, spread, row_weight, picked, hidden,
    result, beside_in, line_out, line_in,
    p_send, p_recv, local_sem, n_send, n_recv, w_send, w_recv, v_send, v_recv, d_send, d_recv,
    g_send, g_recv, zu_send, zu_recv, zd_send, zd_recv, tu_send, tu_recv, td_send, td_recv, f_send, f_recv, y_send, y_recv,
    z_send, z_recv
):
    me, here = lax.axis_index("req"), lax.axis_index("tp")
    beside, across = core_partner(here), (here + 2) % tp_count
    partner = core_partner(me)
    line = req_count // 2
    side, spot = me % 2, me // 2
    moe = arrived
    other = 1 - side
    experts, width, quarter = gate_ref.shape
    pieces = width // columns
    own_rows = tokens_ref.shape[0]
    line_rows = line * own_rows
    f32, bf16 = jnp.float32, jnp.bfloat16
    greet(
        [("tp", beside), ("tp", across), ("req", partner)]
        + [("req", (me + 2 * step) % req_count) for step in range(1, line)]
    )
    second = send_to(partial_ref.at[(beside + 2) % tp_count], pair.at[1], p_send.at[1],
                     p_recv.at[1], "tp", beside)
    second.start()
    first = send_to(partial_ref.at[beside], pair.at[0], p_send.at[0], p_recv.at[0], "tp", beside)
    first.start()

    def part(ref, number, first=0, count=experts):
        return ref.at[first : first + count, :, pl.ds(number * quarter, quarter)]

    def down_part(number):
        return downs.at[:, pl.ds(number * quarter, quarter), :]

    head, rest, inside = weight_plan(experts)
    held = [(gate_ref, gates, 0, 0, experts), (up_ref, ups, 0, 0, experts),
            (gate_head_ref, gates, 1, 0, head)]
    if experts > head:
        held.append((weight_rest_ref.at[: experts - head], gates, 1, head, experts - head))
    if experts > inside:
        held.append((weight_rest_ref.at[experts - head : rest], ups, 1, 0, experts - inside))
    stays = [(ref, part(target, *where)) for ref, target, *where in held]
    goes = [(ref, part(target, number + 2, *where)) for ref, target, number, *where in held]
    stays.append((down_ref, down_part(0)))
    goes.append((down_ref, down_part(2)))
    own_copies = [
        pltpu.make_async_copy(source, target, local_sem.at[i])
        for i, (source, target) in enumerate(stays)
    ]
    near_copies = [
        send_to(source, target, n_send.at[i], n_recv.at[i], "tp", beside)
        for i, (source, target) in enumerate(goes)
    ]

    first_late = experts - inside

    def late_part(place, number):
        return ups.at[first_late + place, :, pl.ds(number * quarter, quarter)]

    late_across = [
        send_to(up_ref.at[first_late + i], late_part(i, 1), w_send.at[i], w_recv.at[i], "tp", across)
        for i in range(inside)
    ]
    late_forward = [
        send_to(late_part(i, 1), late_part(i, 3), v_send.at[i], v_recv.at[i], "tp", beside)
        for i in range(inside)
    ]

    def band(piece):
        return pl.ds(pl.multiple_of(piece * columns, columns), columns)

    def down_across(piece):
        return send_to(down_ref.at[:, :, band(piece)],
                       downs.at[:, pl.ds(quarter, quarter), band(piece)],
                       d_send.at[piece], d_recv.at[piece], "tp", across)

    def down_forward(piece):
        return send_to(downs.at[:, pl.ds(quarter, quarter), band(piece)],
                       downs.at[:, pl.ds(3 * quarter, quarter), band(piece)],
                       g_send.at[piece], g_recv.at[piece], "tp", beside)

    half_rows = own_rows // 2
    halves = [pl.ds(half * half_rows, half_rows) for half in range(2)]
    second.wait()
    lasts = []
    for half, rows in enumerate(halves):
        joined[rows, :] = (
            partial_ref[across, rows, :].astype(f32) + pair[1, rows, :].astype(f32)
        ).astype(bf16)
        copy = send_to(joined.at[rows], far.at[rows], p_send.at[2 + half], p_recv.at[2 + half],
                       "tp", across)
        copy.start()
        lasts.append(copy)
    for copy in late_across:
        copy.start()
    for piece in range(pieces):
        down_across(piece).start()
    first.wait()
    for copy in near_copies + own_copies:
        copy.start()

    def climb(hop, half, block):
        rows = arrived.at[side, block, halves[half]]
        return send_to(rows, rows, zu_send.at[hop, half], zu_recv.at[hop, half], "req",
                       (me + 2) % req_count)

    def descend(hop, half, block):
        rows = arrived.at[side, block, halves[half]]
        return send_to(rows, rows, zd_send.at[hop, half], zd_recv.at[hop, half], "req",
                       (me + req_count - 2) % req_count)

    tail = pl.ds(half_rows + CROSS_ROWS, half_rows - CROSS_ROWS)

    def climb_tail(hop, block):
        rows = arrived.at[other, block, tail]
        return send_to(rows, rows, tu_send.at[hop], tu_recv.at[hop], "req", (me + 2) % req_count)

    def descend_tail(hop, block):
        rows = arrived.at[other, block, tail]
        return send_to(rows, rows, td_send.at[hop], td_recv.at[hop], "req",
                       (me + req_count - 2) % req_count)

    def crossing(from_side, number, half, block):
        short = half == 1 and number > 0
        rows = arrived.at[from_side, block, pl.ds(half_rows, CROSS_ROWS) if short else halves[half]]
        return send_to(rows, rows, f_send.at[number, half], f_recv.at[number, half], "req", partner)

    cross = functools.partial(crossing, side)
    crossed = functools.partial(crossing, other)
    for half, rows in enumerate(halves):
        own = partial_ref[here, rows, :].astype(f32) + pair[0, rows, :].astype(f32)
        own = own + tokens_ref[rows, :].astype(f32)
        lasts[half].wait()
        resid = (own + far[rows, :].astype(f32)).astype(bf16)
        joined[rows, :] = resid
        arrived[side, spot, rows, :] = rms_norm(resid, gain_ref[1:2, :])

        @pl.when(spot < line - 1)
        def _():
            climb(0, half, spot).start()

        @pl.when(spot > 0)
        def _():
            descend(0, half, spot).start()

        cross(0, half, spot).start()

    def prepare(chunk, carry):
        group = (side + chunk) % 2
        place = place_ref[group]
        lane = lax.broadcasted_iota(jnp.int32, (line_rows, experts * slots), 1)
        hit = lane == place[:, 0:1]
        for expert in range(1, experts):
            hit = hit | (lane == place[:, expert : expert + 1])
        spread[chunk] = jnp.where(hit, 1.0, 0.0).astype(bf16)
        for expert in range(experts):
            chosen = (
                lax.broadcasted_iota(jnp.int32, (slots, line_rows), 0) == slot_ref[expert, group]
            )
            pick[chunk, pl.ds(expert * slots, slots), :] = jnp.where(chosen, 1.0, 0.0).astype(bf16)
            row_weight[expert, chunk] = jnp.sum(
                jnp.where(chosen, weight_ref[expert, group], 0.0), axis=1, keepdims=True
            )
        return carry

    lax.fori_loop(0, 2, prepare, 0)
    forwarded = 0
    for hop in range(line - 1):
        for half in range(2):
            @pl.when(spot - 1 - hop >= 0)
            def _():
                block = spot - 1 - hop
                climb(hop, half, block).wait_recv()
                if hop + 1 < line - 1:
                    @pl.when(spot < line - 1)
                    def _():
                        climb(hop + 1, half, block).start()
                cross(1 + hop, half, block).start()

            @pl.when(spot + 1 + hop < line)
            def _():
                block = spot + 1 + hop
                descend(hop, half, block).wait_recv()
                if hop + 1 < line - 1:
                    @pl.when(spot > 0)
                    def _():
                        descend(hop + 1, half, block).start()
                cross(line + hop, half, block).start()

        if hop == 0:
            for half in range(2):
                crossed(0, half, spot).wait_recv()

            @pl.when(spot < line - 1)
            def _():
                climb_tail(0, spot).start()

            @pl.when(spot > 0)
            def _():
                descend_tail(0, spot).start()

        @pl.when(spot - 1 - hop >= 0)
        def _():
            climb_tail(hop, spot - 1 - hop).wait_recv()
            if hop + 1 < line - 1:
                @pl.when(spot < line - 1)
                def _():
                    climb_tail(hop + 1, spot - 1 - hop).start()

        @pl.when(spot + 1 + hop < line)
        def _():
            descend_tail(hop, spot + 1 + hop).wait_recv()
            if hop + 1 < line - 1:
                @pl.when(spot > 0)
                def _():
                    descend_tail(hop + 1, spot + 1 + hop).start()

        if forwarded < inside:
            late_across[forwarded].wait()
            late_forward[forwarded].start()
            forwarded += 1

    def choose(chunk):
        group = (side + chunk) % 2

        def columns_of(piece, carry):
            wide = pl.ds(pl.multiple_of(piece * PICK_COLUMNS, PICK_COLUMNS), PICK_COLUMNS)
            rows = arrived[group, :, :, wide].reshape(line_rows, PICK_COLUMNS)
            values = dot_f32(pick[chunk], rows).astype(bf16)
            for expert in range(experts):
                picked[expert, chunk, :, wide] = values[expert * slots : (expert + 1) * slots]
            return carry

        lax.fori_loop(0, width // PICK_COLUMNS, columns_of, 0)

    def feed(chunk):
        def expert_of(expert, carry):
            rows = picked[expert, chunk]
            gate = dot_f32(rows, gates[expert])
            up = dot_f32(rows, ups[expert])
            hidden[expert, pl.ds(chunk * slots, slots), :] = (jax.nn.silu(gate) * up).astype(bf16)
            return carry

        lax.fori_loop(0, experts, expert_of, 0)

    choose(0)
    for expert in range(forwarded, inside):
        late_across[expert].wait()
        late_forward[expert].start()
    for copy in own_copies + near_copies + late_forward:
        copy.wait()
    feed(0)
    for hop in range(line - 1):
        for half in range(2):
            @pl.when(spot - 1 - hop >= 0)
            def _():
                crossed(1 + hop, half, spot - 1 - hop).wait_recv()

            @pl.when(spot + 1 + hop < line)
            def _():
                crossed(line + hop, half, spot + 1 + hop).wait_recv()

    choose(1)
    feed(1)
    for half in range(2):
        cross(0, half, spot).wait_send()
    for hop in range(line - 1):
        @pl.when((spot < line - 1) & (spot - hop >= 0))
        def _():
            for half in range(2):
                climb(hop, half, spot - hop).wait_send()
            climb_tail(hop, spot - hop).wait_send()

        @pl.when((spot > 0) & (spot + hop < line))
        def _():
            for half in range(2):
                descend(hop, half, spot + hop).wait_send()
            descend_tail(hop, spot + hop).wait_send()

        @pl.when(spot - 1 - hop >= 0)
        def _():
            for half in range(2):
                cross(1 + hop, half, spot - 1 - hop).wait_send()

        @pl.when(spot + 1 + hop < line)
        def _():
            for half in range(2):
                cross(line + hop, half, spot + 1 + hop).wait_send()

    def to_beside(piece):
        return send_to(moe.at[other, :, :, band(piece)], beside_in.at[:, :, band(piece)],
                       y_send.at[piece], y_recv.at[piece], "req", partner)

    def to_line(piece, step):
        return send_to(line_out.at[(spot + step) % line, :, band(piece)],
                       line_in.at[step, :, band(piece)], z_send.at[piece, step],
                       z_recv.at[piece, step], "req", (me + 2 * step) % req_count)

    def finish(piece):
        to_beside(piece).wait()
        line_out[:, :, band(piece)] = (
            moe[side, :, :, band(piece)].astype(f32) + beside_in[:, :, band(piece)].astype(f32)
        ).astype(bf16)
        for step in range(1, line):
            to_line(piece, step).start()

    def relay(piece):
        down_across(piece).wait()
        down_forward(piece).start()

    relay(0)

    def produce(piece, carry):
        down_forward(piece).wait()
        for expert in range(experts):
            values = dot_f32(hidden[expert], downs[expert, :, band(piece)])
            for chunk in range(2):
                result[chunk, pl.ds(expert * slots, slots), :] = (
                    values[chunk * slots : (chunk + 1) * slots] * row_weight[expert, chunk]
                ).astype(bf16)
        for chunk in (1, 0):
            total = dot_f32(spread[chunk], result[chunk]).astype(bf16)
            moe[(side + chunk) % 2, :, :, band(piece)] = total.reshape(line, own_rows, columns)
            if chunk == 1:
                to_beside(piece).start()

        @pl.when(piece + 1 < pieces)
        def _():
            relay(piece + 1)

        @pl.when(piece > 1)
        def _():
            finish(piece - 2)
        return carry

    lax.fori_loop(0, pieces, produce, 0)
    finish(pieces - 2)
    finish(pieces - 1)

    def close(piece, carry):
        total = (
            joined[:, band(piece)].astype(f32) + moe[side, spot, :, band(piece)].astype(f32)
            + beside_in[spot, :, band(piece)].astype(f32)
        )
        for step in range(1, line):
            to_line(piece, step).wait()
            total = total + line_in[step, :, band(piece)].astype(f32)
        out_ref[:, band(piece)] = total.astype(bf16)
        return carry

    lax.fori_loop(0, pieces, close, 0)


def on_device(
    tokens,
    attention_norm_gain,
    expert_norm_gain,
    query_projection,
    key_projection,
    value_projection,
    attention_output_weight,
    cached_keys,
    cached_values,
    token_request,
    cached_request,
    adapter_of_request,
    adapter_table_row,
    adapter_down_maps,
    adapter_query_up,
    adapter_value_up,
    routes,
    routed_weight,
    expert_gate_weight,
    expert_up_weight,
    expert_down_weight,
):
    tp_count = lax.axis_size("tp")
    req_count = lax.axis_size("req")
    req_place = lax.axis_index("req")
    own_rows, width = tokens.shape
    group_size = own_rows * tp_count
    query_width = query_projection.shape[1]
    kv_width = key_projection.shape[1]
    heads = query_width // HEAD_SIZE
    kv_heads = kv_width // HEAD_SIZE
    low_rows = GROUP_REQUESTS * ADAPTER_RANK
    assert tp_count == 4 and kv_heads == 2 and own_rows == QUERY_BLOCK
    capacity = own_rows * TOP // EXPERTS + 2

    in_vmem = pl.BlockSpec(memory_space=pltpu.VMEM)
    in_place = pl.BlockSpec(memory_space=pl.ANY)
    dma = pltpu.SemaphoreType.DMA
    bf16 = jnp.bfloat16
    line = req_count // 2
    part = width // tp_count
    adapter_width = part + query_width + kv_width
    in_smem = pl.BlockSpec(memory_space=pltpu.SMEM)
    vmem = pltpu.VMEM
    f32 = jnp.float32
    half = HEAD_SIZE // 2
    inverse_freq = jnp.asarray(rope_theta ** (-(np.arange(LANES) % half) / half), f32)
    gains = jnp.stack([attention_norm_gain, expert_norm_gain]).astype(f32)
    adapter_block = (line, low_rows, adapter_width)
    head, rest, inside = weight_plan(expert_gate_weight.shape[0])
    head_shape = jax.ShapeDtypeStruct((head,) + expert_gate_weight.shape[1:], bf16)
    rest_shape = jax.ShapeDtypeStruct((max(rest, 1),) + expert_gate_weight.shape[1:], bf16)
    queries, fresh_keys, fresh_values, notes, block_range, edges, bias, gate_head, weight_rest = pl.pallas_call(
        functools.partial(opening_kernel, req_count, tp_count, heads, kv_heads),
        in_specs=[in_place, in_vmem, in_place, in_place, in_place, in_vmem, in_vmem, in_smem,
                  in_smem, in_place, in_place, in_place, in_vmem, in_vmem, in_vmem, in_place, in_place],
        out_specs=[in_vmem] * 7 + [in_place] * 2,
        out_shape=[
            jax.ShapeDtypeStruct((heads, group_size, LANES), bf16),
            jax.ShapeDtypeStruct((group_size, kv_width), bf16),
            jax.ShapeDtypeStruct((group_size, kv_width), bf16),
            jax.ShapeDtypeStruct((req_count, 2 * TOP, own_rows), f32),
            jax.ShapeDtypeStruct((8, LANES), jnp.int32),
            jax.ShapeDtypeStruct((8, LANES), jnp.int32),
            jax.ShapeDtypeStruct((group_size, LANES), bf16),
            head_shape, rest_shape,
        ],
        scratch_shapes=[
            vmem((tp_count, own_rows, width), bf16), vmem((group_size, width), bf16),
            vmem((width, query_width + 2 * kv_width), bf16),
            vmem((adapter_down_maps.shape[0], ADAPTER_RANK, adapter_width), bf16),
            vmem((group_size, query_width), f32), vmem((group_size, kv_width), f32),
            vmem((group_size, LANES), f32), vmem((group_size, LANES), f32),
            vmem((3 * TOP, LANES), f32), vmem((req_count, 3 * TOP, LANES), f32),
            vmem(adapter_block, bf16), vmem(adapter_block, bf16), vmem(adapter_block, bf16),
            vmem(adapter_block, bf16), vmem((low_rows, width), bf16),
            vmem((low_rows, query_width), bf16), vmem((low_rows, kv_width), bf16),
            vmem(rest_shape.shape, bf16),
            dma((7,)), dma((3,)), dma((3,)), dma((req_count,)), dma((req_count,)), dma((line,)),
            dma((line,)), dma((line,)), dma((line,)), dma((3,)), dma((3,)),
            dma((2 * head,)), dma((2 * head,)), dma((rest + 1,)),
        ],
        compiler_params=pltpu.CompilerParams(
            collective_id=1, has_side_effects=True, vmem_limit_bytes=60 << 20
        ),
        cost_estimate=pl.CostEstimate(flops=0, bytes_accessed=300_000_000, transcendentals=0),
        name="opening",
    )(
        tokens, gains, query_projection, key_projection, value_projection,
        token_request, cached_request, adapter_of_request, adapter_table_row, adapter_down_maps,
        adapter_query_up, adapter_value_up, routes.T, routed_weight.T, inverse_freq[None, :],
        expert_gate_weight, expert_up_weight,
    )
    if rest:
        weight_rest = lax.ppermute(weight_rest, "tp", [(i, i ^ 2) for i in range(tp_count)])
    all_routes = notes[:, :TOP].astype(jnp.int32)
    all_gates = notes[:, TOP:]

    whole = lambda shape: pl.BlockSpec(shape, lambda i, *_: (0,) * len(shape))
    by_row = lambda rows, columns: pl.BlockSpec((rows, columns), lambda i, *_: (i, 0))
    context = cached_keys.shape[0]
    partial_rows = pl.pallas_call(
        functools.partial(attention_kernel, heads, kv_heads),
        grid_spec=pltpu.PrefetchScalarGridSpec(
            num_scalar_prefetch=1,
            grid=(group_size // QUERY_BLOCK,),
            in_specs=[
                pl.BlockSpec((heads, QUERY_BLOCK, LANES), lambda i, *_: (0, i, 0)),
                by_row(QUERY_BLOCK, LANES), whole((8, LANES)),
                whole((context, kv_width)), whole((context, kv_width)),
                whole((group_size, kv_width)), whole((group_size, kv_width)),
                whole((query_width, width)),
            ],
            out_specs=by_row(QUERY_BLOCK, width),
        ),
        out_shape=jax.ShapeDtypeStruct((group_size, width), jnp.bfloat16),
        compiler_params=pltpu.CompilerParams(vmem_limit_bytes=56 << 20),
        cost_estimate=pl.CostEstimate(
            flops=0, bytes_accessed=1_000_000, transcendentals=0
        ),
        name="attention",
    )(
        block_range, queries, bias, edges, cached_keys, cached_values, fresh_keys, fresh_values,
        attention_output_weight,
    )
    local_experts, _, quarter = expert_gate_weight.shape
    line_rows = line * own_rows
    slots = -(-line * capacity // 16) * 16
    expert_ids = req_place * local_experts + jnp.arange(local_experts, dtype=jnp.int32)
    hits = all_routes[None] == expert_ids[:, None, None, None]
    expert_weight = jnp.sum(jnp.where(hits, all_gates[None], 0.0), axis=2)
    named = jnp.any(hits, axis=2)
    earlier = jnp.arange(own_rows)[:, None] < jnp.arange(own_rows)[None, :]
    rank = jnp.einsum(
        "ebt,tu->ebu", named.astype(jnp.bfloat16), earlier.astype(jnp.bfloat16),
        preferred_element_type=jnp.float32,
    ).astype(jnp.int32)
    block_base = (jnp.arange(req_count, dtype=jnp.int32) // 2) * capacity

    def by_side(values):
        values = values.reshape(local_experts, line, 2, own_rows)
        return values.transpose(0, 2, 1, 3).reshape(local_experts, 2, line_rows)

    slot_of = by_side(jnp.where(named, rank + block_base[None, :, None], -1))
    expert_weight = by_side(expert_weight)[:, :, None, :]
    expert_base = jnp.arange(local_experts, dtype=jnp.int32) * slots
    place_of = jnp.where(slot_of >= 0, slot_of + expert_base[:, None, None], -1)
    place_of = place_of.transpose(1, 2, 0)
    slot_of = slot_of[:, :, None, :]

    pieces = width // DOWN_COLUMNS
    held = 4 + (local_experts > head) + (local_experts > inside)
    block = (own_rows, width)
    full = 4 * quarter
    return pl.pallas_call(
        functools.partial(moe_kernel, req_count, tp_count, slots, DOWN_COLUMNS),
        in_specs=[in_vmem] * 6 + [in_place] * 5,
        out_specs=in_vmem,
        out_shape=jax.ShapeDtypeStruct(block, bf16),
        scratch_shapes=[
            vmem((2,) + block, bf16), vmem(block, bf16), vmem(block, bf16),
            vmem((2, line) + block, bf16),
            vmem((local_experts, width, full), bf16), vmem((local_experts, width, full), bf16),
            vmem((local_experts, full, width), bf16),
            vmem((2, local_experts * slots, line_rows), bf16),
            vmem((2, line_rows, local_experts * slots), bf16),
            vmem((local_experts, 2, slots, 1), jnp.float32),
            vmem((local_experts, 2, slots, width), bf16),
            vmem((local_experts, 2 * slots, full), bf16),
            vmem((2, local_experts * slots, DOWN_COLUMNS), bf16),
            vmem((line,) + block, bf16), vmem((line,) + block, bf16),
            vmem((line,) + block, bf16),
            dma((4,)), dma((4,)), dma((held,)), dma((held,)), dma((held,)),
            dma((inside,)), dma((inside,)), dma((inside,)), dma((inside,)),
            dma((pieces,)), dma((pieces,)), dma((pieces,)), dma((pieces,)),
            dma((line - 1, 2)), dma((line - 1, 2)), dma((line - 1, 2)), dma((line - 1, 2)),
            dma((line - 1,)), dma((line - 1,)), dma((line - 1,)), dma((line - 1,)),
            dma((2 * line - 1, 2)), dma((2 * line - 1, 2)), dma((pieces,)), dma((pieces,)),
            dma((pieces, line)), dma((pieces, line)),
        ],
        compiler_params=pltpu.CompilerParams(
            collective_id=2, has_side_effects=True, vmem_limit_bytes=60 << 20
        ),
        cost_estimate=pl.CostEstimate(
            flops=0, bytes_accessed=300_000_000, transcendentals=0
        ),
        name="moe",
    )(
        partial_rows.reshape(tp_count, own_rows, width), tokens, gains,
        slot_of, place_of, expert_weight, expert_gate_weight, gate_head, expert_up_weight, weight_rest,
        expert_down_weight,
    )


def solution(mesh):
    return jax.shard_map(
        on_device,
        mesh=mesh,
        in_specs=(
            P(("req", "tp"), None),
            P(),
            P(),
            P(None, "tp"),
            P(None, "tp"),
            P(None, "tp"),
            P("tp", None),
            P("req", "tp"),
            P("req", "tp"),
            P("req", None),
            P("req", None),
            P("req", None),
            P(),
            P("req", None, None),
            P("req", None, "tp"),
            P("req", None, "tp"),
            P("req", None),
            P("req", None),
            P("req", None, "tp"),
            P("req", None, "tp"),
            P("req", "tp", None),
        ),
        out_specs=P(("req", "tp"), None),
        check_vma=False,
    )
```

```python
import functools

import jax
import jax.numpy as jnp
import numpy as np
from jax import lax
from jax.experimental import pallas as pl
from jax.experimental.pallas import tpu as pltpu
from jax.sharding import PartitionSpec as P

HEAD_SIZE = 64
EXPERTS = 32
TOP = 8
ADAPTER_RANK = 16
GROUP_REQUESTS = 4
LANES = 128
KEY_BLOCK = 512
QUERY_BLOCK = 128
HIDDEN_SCORE = -1e30
LOG2_E = 1.4426950408889634
DOWN_COLUMNS = 128
PICK_COLUMNS = 256
CROSS_ROWS = 48

norm_eps = 1e-05
rope_theta = 10000.0


def rms_norm(row_block, gain_row):
    values = row_block.astype(jnp.float32)
    inv_rms = lax.rsqrt(jnp.mean(values * values, axis=-1, keepdims=True) + norm_eps)
    return (values * inv_rms * gain_row).astype(jnp.bfloat16)


def dot_f32(left, right):
    return jnp.dot(left, right, preferred_element_type=jnp.float32)


def attention_kernel(
    heads, kv_heads, range_ref, q_ref, bias_ref, edge_ref, ck_ref, cv_ref, nk_ref, nv_ref, wo_ref,
    out_ref
):
    block = pl.program_id(0)
    rows = q_ref.shape[1]
    queries = jnp.concatenate(
        [q_ref[...].reshape(heads * rows, LANES), jnp.concatenate([bias_ref[...]] * heads, axis=0)],
        axis=1,
    )

    def score(keys, first, edge):
        place = lax.broadcasted_iota(jnp.int32, (keys.shape[0], LANES), 0) + first
        inside = (place >= edge_ref[edge : edge + 1, :]) & (place < edge_ref[edge + 1 : edge + 2, :])
        marks = jnp.where(inside, 1.0, 0.0).astype(jnp.bfloat16)
        return lax.dot_general(
            jnp.concatenate([keys, marks], axis=1), queries, (((1,), (1,)), ((), ())),
            preferred_element_type=jnp.float32,
        )

    def gather(weights, values):
        return lax.dot_general(
            values, weights.astype(jnp.bfloat16), (((0,), (0,)), ((), ())),
            preferred_element_type=jnp.float32,
        )

    def step(keys_ref, values_ref, size, edge, index, carry):
        top, total, mixed = carry
        first = pl.multiple_of(index * size, size)
        scores = score(keys_ref[pl.ds(first, size), :], first, edge)
        new_top = jnp.maximum(top, jnp.max(scores, axis=0, keepdims=True))
        shrink = jnp.exp2(top - new_top)
        weights = jnp.exp2(scores - new_top)
        total = total * shrink + jnp.sum(weights, axis=0, keepdims=True)
        mixed = mixed * shrink + gather(weights, values_ref[pl.ds(first, size), :])
        return new_top, total, mixed

    first = pl.multiple_of(block * rows, rows)
    scores = score(nk_ref[pl.ds(first, rows), :], first, 2)
    key_row = lax.broadcasted_iota(jnp.int32, scores.shape, 0)
    query_row = lax.broadcasted_iota(jnp.int32, scores.shape, 1) % rows
    scores = jnp.where(key_row <= query_row, scores, HIDDEN_SCORE)
    top = jnp.max(scores, axis=0, keepdims=True)
    weights = jnp.exp2(scores - top)
    total = jnp.sum(weights, axis=0, keepdims=True)
    mixed = gather(weights, nv_ref[pl.ds(first, rows), :])
    carry = lax.fori_loop(
        0, block, functools.partial(step, nk_ref, nv_ref, rows, 2), (top, total, mixed)
    )
    top, total, mixed = lax.fori_loop(
        range_ref[0, block], range_ref[1, block],
        functools.partial(step, ck_ref, cv_ref, KEY_BLOCK, 0), carry
    )
    mixed = mixed / total
    per_kv = heads // kv_heads
    pieces = []
    for piece_id in range(heads // 2):
        halves = []
        for head in (2 * piece_id, 2 * piece_id + 1):
            kv = head // per_kv
            halves.append(
                mixed[kv * HEAD_SIZE : (kv + 1) * HEAD_SIZE, head * rows : (head + 1) * rows]
            )
        pieces.append(jnp.transpose(jnp.concatenate(halves, axis=0)).astype(jnp.bfloat16))
    out_ref[...] = dot_f32(jnp.concatenate(pieces, axis=1), wo_ref[...]).astype(jnp.bfloat16)


MESH = pl.DeviceIdType.MESH


def send_to(source, target, send_sem, recv_sem, axis, device):
    return pltpu.make_async_remote_copy(
        src_ref=source, dst_ref=target, send_sem=send_sem, recv_sem=recv_sem,
        device_id={axis: device}, device_id_type=MESH,
    )


def greet(peers):
    barrier = pltpu.get_barrier_semaphore()
    for axis, device in peers:
        pl.semaphore_signal(barrier, inc=1, device_id={axis: device}, device_id_type=MESH)
    pl.semaphore_wait(barrier, len(peers))


def weight_plan(experts):
    head = 1
    rest = min(3, experts - 1)
    return head, rest, 2 * experts - head - rest


def core_partner(place):
    return place + 1 - 2 * (place % 2)


def opening_kernel(
    req_count, tp_count, heads, kv_heads, tokens_ref, gain_ref, wq_ref, wk_ref, wv_ref,
    request_ref, cached_ref, adapter_ref, row_ref, down_ref, qup_ref, vup_ref, routes_ref,
    routed_ref, freq_ref, gate_ref, up_ref, q_ref, k_ref, v_ref, notes_ref, range_ref,
    edge_ref, bias_ref, head_ref, extra_ref, rest_ref,
    group, normed, weights, table, q_part, v_part, cosines, sines, note, noted, near_out,
    near_in, line_out, line_in, downs, qups, vups, bounce,
    local_sem, x_send, x_recv, n_send, n_recv, y_send, y_recv, z_send, z_recv, d_send, d_recv,
    w_send, w_recv, bounce_sem
):
    me, here = lax.axis_index("req"), lax.axis_index("tp")
    beside, across = core_partner(here), (here + 2) % tp_count
    partner = core_partner(me)
    line = req_count // 2
    side, spot = me % 2, me // 2
    other = 1 - side
    f32, bf16 = jnp.float32, jnp.bfloat16
    corner = core_partner(across)
    own_rows, width = tokens_ref.shape
    stored = down_ref.shape[0]
    query_width, kv_width = wq_ref.shape[1], wk_ref.shape[1]
    part = width // tp_count
    edges = (0, part, part + query_width, part + query_width + kv_width)

    own_down = down_ref.at[:, :, pl.ds(pl.multiple_of(here * part, part), part)]
    pieces = [
        (tokens_ref, group.at[here]),
        (own_down, table.at[:, :, edges[0] : edges[1]]),
        (qup_ref, table.at[:, :, edges[1] : edges[2]]),
        (vup_ref, table.at[:, :, edges[2] : edges[3]]),
        (wq_ref, weights.at[:, 0:query_width]),
        (wk_ref, weights.at[:, query_width : query_width + kv_width]),
        (wv_ref, weights.at[:, query_width + kv_width :]),
    ]
    local = [
        pltpu.make_async_copy(source, target, local_sem.at[i])
        for i, (source, target) in enumerate(pieces)
    ]
    experts, depth_all, quarter = gate_ref.shape
    head, rest, _ = weight_plan(experts)
    sources = [gate_ref.at[i] for i in range(experts)] + [up_ref.at[i] for i in range(experts)]
    rest_copies = [
        pltpu.make_async_copy(sources[head + i], bounce.at[i], bounce_sem.at[i])
        for i in range(rest)
    ]
    bounce_copy = pltpu.make_async_copy(bounce, rest_ref, bounce_sem.at[rest])
    head_copies = [
        send_to(source, target, w_send.at[i], w_recv.at[i], "tp", across)
        for i, (source, target) in enumerate([
            (gate_ref.at[pl.ds(0, head)], head_ref),
            (up_ref.at[experts - 1, pl.ds(0, depth_all // 2)], extra_ref),
        ])
    ]
    for copy in local + rest_copies:
        copy.start()
    greet(
        [("req", (me + step) % req_count) for step in range(1, req_count)]
        + [("tp", beside), ("tp", across), ("tp", corner)]
    )
    to_across = send_to(tokens_ref, group.at[here], x_send.at[0], x_recv.at[0], "tp", across)
    to_across.start()
    for copy in head_copies:
        copy.start()

    rows_here = pl.ds(pl.multiple_of(here * own_rows, own_rows), own_rows)
    note[:TOP, :] = routes_ref[:, rows_here].astype(f32)
    note[TOP : 2 * TOP, :] = routed_ref[:, rows_here]
    wanted = [
        jnp.full((1, LANES), row_ref[adapter_ref[0, i]], jnp.int32) for i in range(GROUP_REQUESTS)
    ]
    note[2 * TOP :, :] = jnp.concatenate(wanted + wanted, axis=0).astype(f32)

    def tell(step):
        return send_to(note, noted.at[me], n_send.at[step], n_recv.at[me], "req",
                       (me + step) % req_count)

    def told(source):
        return send_to(note, noted.at[source], n_send.at[0], n_recv.at[source], "req", partner)

    for step in range(1, req_count):
        tell(step).start()
    to_beside = send_to(tokens_ref, group.at[here], x_send.at[1], x_recv.at[1], "tp", beside)
    to_beside.start()
    noted[me] = note[...]

    labels = request_ref[...]
    old_labels = cached_ref[...]

    def count(mask):
        return jnp.sum(jnp.where(mask, 1.0, 0.0), axis=1, keepdims=True).astype(jnp.int32)

    new_below = [count(labels < i) for i in range(GROUP_REQUESTS)]
    old_below = [count(old_labels < i) for i in range(GROUP_REQUESTS + 1)]
    new_below.append(count(labels < GROUP_REQUESTS))
    column = lax.broadcasted_iota(jnp.int32, (1, LANES), 1)
    edges_of = []
    for below in (old_below, new_below):
        low_edge = jnp.zeros_like(column)
        high_edge = jnp.zeros_like(column)
        for i in range(GROUP_REQUESTS):
            low_edge = jnp.where(column == i, below[i], low_edge)
            high_edge = jnp.where(column == i, below[i + 1], high_edge)
        edges_of += [low_edge, high_edge]
    edge_ref[...] = jnp.concatenate(edges_of * 2, axis=0)
    old_start, old_end = jnp.zeros_like(labels), jnp.zeros_like(labels)
    for i in range(GROUP_REQUESTS):
        member = labels == i
        old_start = jnp.where(member, old_below[i], old_start)
        old_end = jnp.where(member, old_below[i + 1], old_end)
    starts, ends = jnp.zeros_like(column), jnp.zeros_like(column)
    for i in range(tp_count):
        block = slice(i * own_rows, (i + 1) * own_rows)
        start = jnp.min(old_start[:, block].astype(f32), axis=1, keepdims=True).astype(jnp.int32)
        end = jnp.max(old_end[:, block].astype(f32), axis=1, keepdims=True).astype(jnp.int32)
        starts = jnp.where(column == i, start // KEY_BLOCK, starts)
        ends = jnp.where(column == i, (end + KEY_BLOCK - 1) // KEY_BLOCK, ends)
    range_ref[...] = jnp.concatenate([starts, ends] * 4, axis=0)
    place = lax.broadcasted_iota(jnp.int32, (tp_count * own_rows, LANES), 0)
    moved = jnp.zeros_like(place)
    request = jnp.zeros_like(place)
    for i in range(GROUP_REQUESTS):
        offset = old_below[i + 1] - old_below[i] - new_below[i]
        moved = jnp.where(place >= new_below[i], offset, moved)
        request = jnp.where(place >= new_below[i], i, request)
    label = lax.broadcasted_iota(jnp.int32, place.shape, 1)
    hidden_pair = (label < GROUP_REQUESTS) & (label != request)
    bias_ref[...] = jnp.where(hidden_pair, HIDDEN_SCORE, 0.0).astype(bf16)
    lane = lax.broadcasted_iota(jnp.int32, (2 * own_rows, LANES), 1)
    front = lane % HEAD_SIZE < HEAD_SIZE // 2
    upper = lane >= HEAD_SIZE
    low_rows = GROUP_REQUESTS * ADAPTER_RANK
    depth = stored * ADAPTER_RANK
    column = lax.broadcasted_iota(jnp.int32, (low_rows, depth), 1)
    row = lax.broadcasted_iota(jnp.int32, (low_rows, depth), 0)
    same_rank = column % ADAPTER_RANK == row % ADAPTER_RANK
    slot = (me * stored + column // ADAPTER_RANK).astype(f32)

    def select(source):
        rows = [
            jnp.broadcast_to(noted[source, pl.ds(2 * TOP + i, 1), :], (ADAPTER_RANK, LANES))
            for i in range(GROUP_REQUESTS)
        ]
        sought = jnp.concatenate(rows, axis=0)[:, :depth]
        pick = jnp.where(same_rank & (sought == slot), 1.0, 0.0).astype(bf16)
        return dot_f32(pick, table[...].reshape(depth, edges[3]))

    def to_near(goal):
        return send_to(near_out.at[goal], near_in.at[goal], y_send.at[goal], y_recv.at[goal],
                       "req", partner)

    def to_line(step):
        return send_to(line_out.at[step], line_in.at[step], z_send.at[step], z_recv.at[step],
                       "req", (me + 2 * step) % req_count)

    for copy in local[1:4]:
        copy.wait()
    for step in list(range(1, line)) + [0]:
        goal = (spot + step) % line
        told(2 * goal + other).wait_recv()
        near_out[goal] = select(2 * goal + other).astype(bf16)
        to_near(goal).start()

    angles = (place + moved).astype(f32) * freq_ref[...]
    cosines[...] = jnp.cos(angles)
    sines[...] = jnp.sin(angles)

    def turn(piece, rows):
        rolled = jnp.where(
            front,
            -pltpu.roll(piece, LANES - HEAD_SIZE // 2, 1),
            pltpu.roll(piece, HEAD_SIZE // 2, 1),
        )
        return piece * cosines[rows, :] + rolled * sines[rows, :]

    def rows_of(pair):
        return pl.ds(pl.multiple_of(pair * 2 * own_rows, 2 * own_rows), 2 * own_rows)

    def project(pair):
        rows = rows_of(pair)
        values = rms_norm(group[pl.ds(2 * pair, 2)].reshape(2 * own_rows, width), gain_ref[...].astype(f32)[None, :])
        normed[rows, :] = values
        product = dot_f32(values, weights[...])
        q_part[rows, :] = product[:, :query_width]
        k_ref[rows, :] = turn(product[:, query_width : query_width + kv_width], rows).astype(bf16)
        v_part[rows, :] = product[:, query_width + kv_width :]

    own_pair = here // 2
    for copy in rest_copies:
        copy.wait()
    bounce_copy.start()
    local[0].wait()
    for copy in local[4:]:
        copy.wait()
    to_beside.wait()
    forward = send_to(group.at[across], group.at[across], x_send.at[2], x_recv.at[2], "tp", beside)
    for step in range(1, line):
        goal = (spot + step) % line
        to_near(goal).wait_recv()
        told(2 * goal + side).wait_recv()
        line_out[step] = (select(2 * goal + side) + near_in[goal].astype(f32)).astype(bf16)
        to_line(step).start()
        if step == 1:
            project(own_pair)
        if step == min(2, line - 1):
            to_across.wait()
            forward.start()
    forward.wait()
    project(1 - own_pair)
    to_near(spot).wait_recv()
    for source in range(req_count):
        notes_ref[source] = noted[source, : 2 * TOP, :]
    total = select(me) + near_in[spot].astype(f32)
    for step in range(1, line):
        to_line(step).wait_recv()
        total = total + line_in[step].astype(f32)
    total = total.astype(bf16)

    def down_columns(owner):
        return downs.at[:, pl.ds(pl.multiple_of(owner * part, part), part)]

    downs[:, pl.ds(pl.multiple_of(here * part, part), part)] = total[:, edges[0] : edges[1]]
    down_copies = [
        send_to(down_columns(here), down_columns(here), d_send.at[i], d_recv.at[i], "tp", device)
        for i, device in enumerate((across, corner, beside))
    ]
    for copy in down_copies:
        copy.start()
    qups[...] = total[:, edges[1] : edges[2]]
    vups[...] = total[:, edges[2] : edges[3]]
    for copy in down_copies:
        copy.wait()
    per_kv = heads // kv_heads

    def complete(pair, carry):
        rows = rows_of(pair)
        low = lax.dot_general(
            downs[...], normed[rows, :], (((1,), (1,)), ((), ())), preferred_element_type=f32
        )
        owner = lax.broadcasted_iota(jnp.int32, low.shape, 0) // ADAPTER_RANK
        low = jnp.where(owner == request_ref[:, rows], low, 0.0).astype(bf16)

        def raised(ups):
            return lax.dot_general(
                low, ups, (((0,), (0,)), ((), ())), preferred_element_type=f32
            )

        v_ref[rows, :] = (v_part[rows, :] + raised(vups[...])).astype(bf16)
        q = q_part[rows, :] + raised(qups[...])
        for piece_id in range(heads // 2):
            turned = turn(q[:, piece_id * LANES : (piece_id + 1) * LANES], rows)
            turned = turned * (HEAD_SIZE ** (-0.5) * LOG2_E)
            swapped = pltpu.roll(turned, HEAD_SIZE, 1)
            for half in range(2):
                head = 2 * piece_id + half
                kv = head // per_kv
                source = turned if kv == half else swapped
                keep = upper if kv == 1 else jnp.logical_not(upper)
                q_ref[head, rows, :] = jnp.where(keep, source, 0.0).astype(bf16)
        return carry

    lax.fori_loop(0, 2, complete, 0)
    for copy in head_copies:
        copy.wait()
    bounce_copy.wait()
    for step in range(1, req_count):
        tell(step).wait_send()
    for step in range(line):
        to_near((spot + step) % line).wait_send()
    for step in range(1, line):
        to_line(step).wait_send()


def moe_kernel(
    req_count, tp_count, slots, columns, partial_ref, tokens_ref, gain_ref, slot_ref,
    place_ref, weight_ref, gate_ref, gate_head_ref, up_ref, up_extra_ref, weight_rest_ref, down_ref,
    out_ref,
    pair, mine, rest_tokens, joined, far, arrived, gates, ups, downs, pick, spread, row_weight, picked, hidden,
    result, beside_in, line_out, line_in,
    early_sem, p_send, p_recv, local_sem, n_send, n_recv, w_send, w_recv, v_send, v_recv, d_send, d_recv,
    g_send, g_recv, zu_send, zu_recv, zd_send, zd_recv, tu_send, tu_recv, td_send, td_recv, f_send, f_recv, y_send, y_recv,
    z_send, z_recv
):
    me, here = lax.axis_index("req"), lax.axis_index("tp")
    beside, across = core_partner(here), (here + 2) % tp_count
    partner = core_partner(me)
    line = req_count // 2
    side, spot = me % 2, me // 2
    moe = arrived
    other = 1 - side
    experts, width, quarter = gate_ref.shape
    pieces = width // columns
    own_rows = tokens_ref.shape[0]
    line_rows = line * own_rows
    f32, bf16 = jnp.float32, jnp.bfloat16
    early = [
        pltpu.make_async_copy(partial_ref.at[across], mine.at[0], early_sem.at[0]),
        pltpu.make_async_copy(partial_ref.at[here], mine.at[1], early_sem.at[1]),
        pltpu.make_async_copy(tokens_ref, rest_tokens, early_sem.at[2]),
    ]
    for copy in early:
        copy.start()
    greet(
        [("tp", beside), ("tp", across), ("req", partner)]
        + [("req", (me + 2 * step) % req_count) for step in range(1, line)]
    )
    second = send_to(partial_ref.at[(beside + 2) % tp_count], pair.at[1], p_send.at[1],
                     p_recv.at[1], "tp", beside)
    second.start()
    first = send_to(partial_ref.at[beside], pair.at[0], p_send.at[0], p_recv.at[0], "tp", beside)
    first.start()

    def part(ref, number, first=0, count=experts):
        return ref.at[first : first + count, :, pl.ds(number * quarter, quarter)]

    def down_part(number):
        return downs.at[:, pl.ds(number * quarter, quarter), :]

    head, rest, inside = weight_plan(experts)
    held = [(gate_ref, gates, 0, 0, experts), (up_ref, ups, 0, 0, experts),
            (gate_head_ref, gates, 1, 0, head)]
    if experts > head:
        held.append((weight_rest_ref.at[: experts - head], gates, 1, head, experts - head))
    if experts > inside:
        held.append((weight_rest_ref.at[experts - head : rest], ups, 1, 0, experts - inside))
    stays = [(ref, part(target, *where)) for ref, target, *where in held]
    goes = [(ref, part(target, number + 2, *where)) for ref, target, number, *where in held]
    sent = width // 2

    def extra_part(number):
        return ups.at[experts - 1, pl.ds(0, sent), pl.ds(number * quarter, quarter)]

    stays += [(up_extra_ref, extra_part(1)), (down_ref, down_part(0))]
    goes += [(up_extra_ref, extra_part(3)), (down_ref, down_part(2))]
    own_copies = [
        pltpu.make_async_copy(source, target, local_sem.at[i])
        for i, (source, target) in enumerate(stays)
    ]
    near_copies = [
        send_to(source, target, n_send.at[i], n_recv.at[i], "tp", beside)
        for i, (source, target) in enumerate(goes)
    ]

    first_late = experts - inside

    def late_rows(place):
        return pl.ds(sent, width - sent) if place == inside - 1 else pl.ds(0, width)

    def late_part(place, number):
        return ups.at[first_late + place, late_rows(place), pl.ds(number * quarter, quarter)]

    late_across = [
        send_to(up_ref.at[first_late + i, late_rows(i)], late_part(i, 1), w_send.at[i],
                w_recv.at[i], "tp", across)
        for i in range(inside)
    ]
    late_forward = [
        send_to(late_part(i, 1), late_part(i, 3), v_send.at[i], v_recv.at[i], "tp", beside)
        for i in range(inside)
    ]

    def band(piece):
        return pl.ds(pl.multiple_of(piece * columns, columns), columns)

    def down_across(piece):
        return send_to(down_ref.at[:, :, band(piece)],
                       downs.at[:, pl.ds(quarter, quarter), band(piece)],
                       d_send.at[piece], d_recv.at[piece], "tp", across)

    def down_forward(piece):
        return send_to(downs.at[:, pl.ds(quarter, quarter), band(piece)],
                       downs.at[:, pl.ds(3 * quarter, quarter), band(piece)],
                       g_send.at[piece], g_recv.at[piece], "tp", beside)

    half_rows = own_rows // 2
    halves = [pl.ds(half * half_rows, half_rows) for half in range(2)]
    early[0].wait()
    second.wait()
    lasts = []
    for half, rows in enumerate(halves):
        joined[rows, :] = (
            mine[0, rows, :].astype(f32) + pair[1, rows, :].astype(f32)
        ).astype(bf16)
        copy = send_to(joined.at[rows], far.at[rows], p_send.at[2 + half], p_recv.at[2 + half],
                       "tp", across)
        copy.start()
        lasts.append(copy)
    for copy in late_across:
        copy.start()
    for piece in range(pieces):
        down_across(piece).start()
    first.wait()
    for copy in early[1:]:
        copy.wait()
    for copy in near_copies + own_copies:
        copy.start()

    def climb(hop, half, block):
        rows = arrived.at[side, block, halves[half]]
        return send_to(rows, rows, zu_send.at[hop, half], zu_recv.at[hop, half], "req",
                       (me + 2) % req_count)

    def descend(hop, half, block):
        rows = arrived.at[side, block, halves[half]]
        return send_to(rows, rows, zd_send.at[hop, half], zd_recv.at[hop, half], "req",
                       (me + req_count - 2) % req_count)

    tail = pl.ds(half_rows + CROSS_ROWS, half_rows - CROSS_ROWS)

    def climb_tail(hop, block):
        rows = arrived.at[other, block, tail]
        return send_to(rows, rows, tu_send.at[hop], tu_recv.at[hop], "req", (me + 2) % req_count)

    def descend_tail(hop, block):
        rows = arrived.at[other, block, tail]
        return send_to(rows, rows, td_send.at[hop], td_recv.at[hop], "req",
                       (me + req_count - 2) % req_count)

    def crossing(from_side, number, half, block):
        short = half == 1 and number > 0
        rows = arrived.at[from_side, block, pl.ds(half_rows, CROSS_ROWS) if short else halves[half]]
        return send_to(rows, rows, f_send.at[number, half], f_recv.at[number, half], "req", partner)

    cross = functools.partial(crossing, side)
    crossed = functools.partial(crossing, other)
    for half, rows in enumerate(halves):
        own = mine[1, rows, :].astype(f32) + pair[0, rows, :].astype(f32)
        own = own + rest_tokens[rows, :].astype(f32)
        lasts[half].wait()
        resid = (own + far[rows, :].astype(f32)).astype(bf16)
        joined[rows, :] = resid
        arrived[side, spot, rows, :] = rms_norm(resid, gain_ref[...].astype(f32)[None, :])

        @pl.when(spot < line - 1)
        def _():
            climb(0, half, spot).start()

        @pl.when(spot > 0)
        def _():
            descend(0, half, spot).start()

        cross(0, half, spot).start()

    def prepare(chunk, carry):
        group = (side + chunk) % 2
        place = place_ref[group]
        lane = lax.broadcasted_iota(jnp.int32, (line_rows, experts * slots), 1)
        hit = lane == place[:, 0:1]
        for expert in range(1, experts):
            hit = hit | (lane == place[:, expert : expert + 1])
        spread[chunk] = jnp.where(hit, 1.0, 0.0).astype(bf16)
        for expert in range(experts):
            chosen = (
                lax.broadcasted_iota(jnp.int32, (slots, line_rows), 0) == slot_ref[expert, group]
            )
            pick[chunk, pl.ds(expert * slots, slots), :] = jnp.where(chosen, 1.0, 0.0).astype(bf16)
            row_weight[expert, chunk] = jnp.sum(
                jnp.where(chosen, weight_ref[expert, group], 0.0), axis=1, keepdims=True
            )
        return carry

    lax.fori_loop(0, 2, prepare, 0)
    forwarded = 0
    for hop in range(line - 1):
        for half in range(2):
            @pl.when(spot - 1 - hop >= 0)
            def _():
                block = spot - 1 - hop
                climb(hop, half, block).wait_recv()
                if hop + 1 < line - 1:
                    @pl.when(spot < line - 1)
                    def _():
                        climb(hop + 1, half, block).start()
                cross(1 + hop, half, block).start()

            @pl.when(spot + 1 + hop < line)
            def _():
                block = spot + 1 + hop
                descend(hop, half, block).wait_recv()
                if hop + 1 < line - 1:
                    @pl.when(spot > 0)
                    def _():
                        descend(hop + 1, half, block).start()
                cross(line + hop, half, block).start()

        if hop == 0:
            for half in range(2):
                crossed(0, half, spot).wait_recv()

            @pl.when(spot < line - 1)
            def _():
                climb_tail(0, spot).start()

            @pl.when(spot > 0)
            def _():
                descend_tail(0, spot).start()

        @pl.when(spot - 1 - hop >= 0)
        def _():
            climb_tail(hop, spot - 1 - hop).wait_recv()
            if hop + 1 < line - 1:
                @pl.when(spot < line - 1)
                def _():
                    climb_tail(hop + 1, spot - 1 - hop).start()

        @pl.when(spot + 1 + hop < line)
        def _():
            descend_tail(hop, spot + 1 + hop).wait_recv()
            if hop + 1 < line - 1:
                @pl.when(spot > 0)
                def _():
                    descend_tail(hop + 1, spot + 1 + hop).start()

        if forwarded < inside:
            late_across[forwarded].wait()
            late_forward[forwarded].start()
            forwarded += 1

    def choose(chunk):
        group = (side + chunk) % 2

        def columns_of(piece, carry):
            wide = pl.ds(pl.multiple_of(piece * PICK_COLUMNS, PICK_COLUMNS), PICK_COLUMNS)
            rows = arrived[group, :, :, wide].reshape(line_rows, PICK_COLUMNS)
            values = dot_f32(pick[chunk], rows).astype(bf16)
            for expert in range(experts):
                picked[expert, chunk, :, wide] = values[expert * slots : (expert + 1) * slots]
            return carry

        lax.fori_loop(0, width // PICK_COLUMNS, columns_of, 0)

    def feed(chunk):
        def expert_of(expert, carry):
            rows = picked[expert, chunk]
            gate = dot_f32(rows, gates[expert])
            up = dot_f32(rows, ups[expert])
            hidden[expert, pl.ds(chunk * slots, slots), :] = (jax.nn.silu(gate) * up).astype(bf16)
            return carry

        lax.fori_loop(0, experts, expert_of, 0)

    choose(0)
    for expert in range(forwarded, inside):
        late_across[expert].wait()
        late_forward[expert].start()
    for copy in own_copies + near_copies + late_forward:
        copy.wait()
    feed(0)
    for hop in range(line - 1):
        for half in range(2):
            @pl.when(spot - 1 - hop >= 0)
            def _():
                crossed(1 + hop, half, spot - 1 - hop).wait_recv()

            @pl.when(spot + 1 + hop < line)
            def _():
                crossed(line + hop, half, spot + 1 + hop).wait_recv()

    choose(1)
    feed(1)
    for half in range(2):
        cross(0, half, spot).wait_send()
    for hop in range(line - 1):
        @pl.when((spot < line - 1) & (spot - hop >= 0))
        def _():
            for half in range(2):
                climb(hop, half, spot - hop).wait_send()
            climb_tail(hop, spot - hop).wait_send()

        @pl.when((spot > 0) & (spot + hop < line))
        def _():
            for half in range(2):
                descend(hop, half, spot + hop).wait_send()
            descend_tail(hop, spot + hop).wait_send()

        @pl.when(spot - 1 - hop >= 0)
        def _():
            for half in range(2):
                cross(1 + hop, half, spot - 1 - hop).wait_send()

        @pl.when(spot + 1 + hop < line)
        def _():
            for half in range(2):
                cross(line + hop, half, spot + 1 + hop).wait_send()

    def to_beside(piece):
        return send_to(moe.at[other, :, :, band(piece)], beside_in.at[:, :, band(piece)],
                       y_send.at[piece], y_recv.at[piece], "req", partner)

    def to_line(piece, step):
        return send_to(line_out.at[(spot + step) % line, :, band(piece)],
                       line_in.at[step, :, band(piece)], z_send.at[piece, step],
                       z_recv.at[piece, step], "req", (me + 2 * step) % req_count)

    def finish(piece):
        to_beside(piece).wait()
        line_out[:, :, band(piece)] = (
            moe[side, :, :, band(piece)].astype(f32) + beside_in[:, :, band(piece)].astype(f32)
        ).astype(bf16)
        for step in range(1, line):
            to_line(piece, step).start()

    def relay(piece):
        down_across(piece).wait()
        down_forward(piece).start()

    relay(0)

    def produce(piece, carry):
        down_forward(piece).wait()
        for expert in range(experts):
            values = dot_f32(hidden[expert], downs[expert, :, band(piece)])
            for chunk in range(2):
                result[chunk, pl.ds(expert * slots, slots), :] = (
                    values[chunk * slots : (chunk + 1) * slots] * row_weight[expert, chunk]
                ).astype(bf16)
        for chunk in (1, 0):
            total = dot_f32(spread[chunk], result[chunk]).astype(bf16)
            moe[(side + chunk) % 2, :, :, band(piece)] = total.reshape(line, own_rows, columns)
            if chunk == 1:
                to_beside(piece).start()

        @pl.when(piece + 1 < pieces)
        def _():
            relay(piece + 1)

        @pl.when(piece > 1)
        def _():
            finish(piece - 2)
        return carry

    lax.fori_loop(0, pieces, produce, 0)
    finish(pieces - 2)
    finish(pieces - 1)

    def close(piece, carry):
        total = (
            joined[:, band(piece)].astype(f32) + moe[side, spot, :, band(piece)].astype(f32)
            + beside_in[spot, :, band(piece)].astype(f32)
        )
        for step in range(1, line):
            to_line(piece, step).wait()
            total = total + line_in[step, :, band(piece)].astype(f32)
        out_ref[:, band(piece)] = total.astype(bf16)
        return carry

    lax.fori_loop(0, pieces, close, 0)


def on_device(
    tokens,
    attention_norm_gain,
    expert_norm_gain,
    query_projection,
    key_projection,
    value_projection,
    attention_output_weight,
    cached_keys,
    cached_values,
    token_request,
    cached_request,
    adapter_of_request,
    adapter_table_row,
    adapter_down_maps,
    adapter_query_up,
    adapter_value_up,
    routes,
    routed_weight,
    expert_gate_weight,
    expert_up_weight,
    expert_down_weight,
):
    tp_count = lax.axis_size("tp")
    req_count = lax.axis_size("req")
    req_place = lax.axis_index("req")
    own_rows, width = tokens.shape
    group_size = own_rows * tp_count
    query_width = query_projection.shape[1]
    kv_width = key_projection.shape[1]
    heads = query_width // HEAD_SIZE
    kv_heads = kv_width // HEAD_SIZE
    low_rows = GROUP_REQUESTS * ADAPTER_RANK
    assert tp_count == 4 and kv_heads == 2 and own_rows == QUERY_BLOCK
    capacity = own_rows * TOP // EXPERTS + 2

    in_vmem = pl.BlockSpec(memory_space=pltpu.VMEM)
    in_place = pl.BlockSpec(memory_space=pl.ANY)
    dma = pltpu.SemaphoreType.DMA
    bf16 = jnp.bfloat16
    line = req_count // 2
    part = width // tp_count
    adapter_width = part + query_width + kv_width
    in_smem = pl.BlockSpec(memory_space=pltpu.SMEM)
    vmem = pltpu.VMEM
    f32 = jnp.float32
    half = HEAD_SIZE // 2
    inverse_freq = jnp.asarray(rope_theta ** (-(np.arange(LANES) % half) / half), f32)
    adapter_block = (line, low_rows, adapter_width)
    head, rest, inside = weight_plan(expert_gate_weight.shape[0])
    extra_shape = jax.ShapeDtypeStruct((width // 2, expert_gate_weight.shape[2]), bf16)
    head_shape = jax.ShapeDtypeStruct((head,) + expert_gate_weight.shape[1:], bf16)
    rest_shape = jax.ShapeDtypeStruct((max(rest, 1),) + expert_gate_weight.shape[1:], bf16)
    queries, fresh_keys, fresh_values, notes, block_range, edges, bias, gate_head, up_extra, weight_rest = pl.pallas_call(
        functools.partial(opening_kernel, req_count, tp_count, heads, kv_heads),
        in_specs=[in_place, in_vmem, in_place, in_place, in_place, in_vmem, in_vmem, in_smem,
                  in_smem, in_place, in_place, in_place, in_vmem, in_vmem, in_vmem, in_place, in_place],
        out_specs=[in_vmem] * 7 + [in_place] * 3,
        out_shape=[
            jax.ShapeDtypeStruct((heads, group_size, LANES), bf16),
            jax.ShapeDtypeStruct((group_size, kv_width), bf16),
            jax.ShapeDtypeStruct((group_size, kv_width), bf16),
            jax.ShapeDtypeStruct((req_count, 2 * TOP, own_rows), f32),
            jax.ShapeDtypeStruct((8, LANES), jnp.int32),
            jax.ShapeDtypeStruct((8, LANES), jnp.int32),
            jax.ShapeDtypeStruct((group_size, LANES), bf16),
            head_shape, extra_shape, rest_shape,
        ],
        scratch_shapes=[
            vmem((tp_count, own_rows, width), bf16), vmem((group_size, width), bf16),
            vmem((width, query_width + 2 * kv_width), bf16),
            vmem((adapter_down_maps.shape[0], ADAPTER_RANK, adapter_width), bf16),
            vmem((group_size, query_width), f32), vmem((group_size, kv_width), f32),
            vmem((group_size, LANES), f32), vmem((group_size, LANES), f32),
            vmem((3 * TOP, LANES), f32), vmem((req_count, 3 * TOP, LANES), f32),
            vmem(adapter_block, bf16), vmem(adapter_block, bf16), vmem(adapter_block, bf16),
            vmem(adapter_block, bf16), vmem((low_rows, width), bf16),
            vmem((low_rows, query_width), bf16), vmem((low_rows, kv_width), bf16),
            vmem(rest_shape.shape, bf16),
            dma((7,)), dma((3,)), dma((3,)), dma((req_count,)), dma((req_count,)), dma((line,)),
            dma((line,)), dma((line,)), dma((line,)), dma((3,)), dma((3,)),
            dma((2,)), dma((2,)), dma((rest + 1,)),
        ],
        compiler_params=pltpu.CompilerParams(
            collective_id=1, has_side_effects=True, vmem_limit_bytes=60 << 20
        ),
        cost_estimate=pl.CostEstimate(flops=0, bytes_accessed=300_000_000, transcendentals=0),
        name="opening",
    )(
        tokens, attention_norm_gain, query_projection, key_projection, value_projection,
        token_request, cached_request, adapter_of_request, adapter_table_row, adapter_down_maps,
        adapter_query_up, adapter_value_up, routes.T, routed_weight.T, inverse_freq[None, :],
        expert_gate_weight, expert_up_weight,
    )
    if rest:
        weight_rest = lax.ppermute(weight_rest, "tp", [(i, i ^ 2) for i in range(tp_count)])
    all_routes = notes[:, :TOP].astype(jnp.int32)
    all_gates = notes[:, TOP:]

    whole = lambda shape: pl.BlockSpec(shape, lambda i, *_: (0,) * len(shape))
    by_row = lambda rows, columns: pl.BlockSpec((rows, columns), lambda i, *_: (i, 0))
    context = cached_keys.shape[0]
    partial_rows = pl.pallas_call(
        functools.partial(attention_kernel, heads, kv_heads),
        grid_spec=pltpu.PrefetchScalarGridSpec(
            num_scalar_prefetch=1,
            grid=(group_size // QUERY_BLOCK,),
            in_specs=[
                pl.BlockSpec((heads, QUERY_BLOCK, LANES), lambda i, *_: (0, i, 0)),
                by_row(QUERY_BLOCK, LANES), whole((8, LANES)),
                whole((context, kv_width)), whole((context, kv_width)),
                whole((group_size, kv_width)), whole((group_size, kv_width)),
                whole((query_width, width)),
            ],
            out_specs=by_row(QUERY_BLOCK, width),
        ),
        out_shape=jax.ShapeDtypeStruct((group_size, width), jnp.bfloat16),
        compiler_params=pltpu.CompilerParams(vmem_limit_bytes=63 << 20),
        cost_estimate=pl.CostEstimate(
            flops=0, bytes_accessed=1_000_000, transcendentals=0
        ),
        name="attention",
    )(
        block_range, queries, bias, edges, cached_keys, cached_values, fresh_keys, fresh_values,
        attention_output_weight,
    )
    local_experts, _, quarter = expert_gate_weight.shape
    line_rows = line * own_rows
    slots = -(-line * capacity // 16) * 16
    expert_ids = req_place * local_experts + jnp.arange(local_experts, dtype=jnp.int32)
    hits = all_routes[None] == expert_ids[:, None, None, None]
    expert_weight = jnp.sum(jnp.where(hits, all_gates[None], 0.0), axis=2)
    named = jnp.any(hits, axis=2)
    earlier = jnp.arange(own_rows)[:, None] < jnp.arange(own_rows)[None, :]
    rank = jnp.einsum(
        "ebt,tu->ebu", named.astype(jnp.bfloat16), earlier.astype(jnp.bfloat16),
        preferred_element_type=jnp.float32,
    ).astype(jnp.int32)
    block_base = (jnp.arange(req_count, dtype=jnp.int32) // 2) * capacity

    def by_side(values):
        values = values.reshape(local_experts, line, 2, own_rows)
        return values.transpose(0, 2, 1, 3).reshape(local_experts, 2, line_rows)

    slot_of = by_side(jnp.where(named, rank + block_base[None, :, None], -1))
    expert_weight = by_side(expert_weight)[:, :, None, :]
    expert_base = jnp.arange(local_experts, dtype=jnp.int32) * slots
    place_of = jnp.where(slot_of >= 0, slot_of + expert_base[:, None, None], -1)
    place_of = place_of.transpose(1, 2, 0)
    slot_of = slot_of[:, :, None, :]

    pieces = width // DOWN_COLUMNS
    held = 5 + (local_experts > head) + (local_experts > inside)
    block = (own_rows, width)
    full = 4 * quarter
    return pl.pallas_call(
        functools.partial(moe_kernel, req_count, tp_count, slots, DOWN_COLUMNS),
        in_specs=[in_place] * 2 + [in_vmem] * 4 + [in_place] * 6,
        out_specs=in_vmem,
        out_shape=jax.ShapeDtypeStruct(block, bf16),
        scratch_shapes=[
            vmem((2,) + block, bf16), vmem((2,) + block, bf16), vmem(block, bf16),
            vmem(block, bf16), vmem(block, bf16),
            vmem((2, line) + block, bf16),
            vmem((local_experts, width, full), bf16), vmem((local_experts, width, full), bf16),
            vmem((local_experts, full, width), bf16),
            vmem((2, local_experts * slots, line_rows), bf16),
            vmem((2, line_rows, local_experts * slots), bf16),
            vmem((local_experts, 2, slots, 1), jnp.float32),
            vmem((local_experts, 2, slots, width), bf16),
            vmem((local_experts, 2 * slots, full), bf16),
            vmem((2, local_experts * slots, DOWN_COLUMNS), bf16),
            vmem((line,) + block, bf16), vmem((line,) + block, bf16),
            vmem((line,) + block, bf16),
            dma((3,)), dma((4,)), dma((4,)), dma((held,)), dma((held,)), dma((held,)),
            dma((inside,)), dma((inside,)), dma((inside,)), dma((inside,)),
            dma((pieces,)), dma((pieces,)), dma((pieces,)), dma((pieces,)),
            dma((line - 1, 2)), dma((line - 1, 2)), dma((line - 1, 2)), dma((line - 1, 2)),
            dma((line - 1,)), dma((line - 1,)), dma((line - 1,)), dma((line - 1,)),
            dma((2 * line - 1, 2)), dma((2 * line - 1, 2)), dma((pieces,)), dma((pieces,)),
            dma((pieces, line)), dma((pieces, line)),
        ],
        compiler_params=pltpu.CompilerParams(
            collective_id=2, has_side_effects=True, vmem_limit_bytes=60 << 20
        ),
        cost_estimate=pl.CostEstimate(
            flops=0, bytes_accessed=300_000_000, transcendentals=0
        ),
        name="moe",
    )(
        partial_rows.reshape(tp_count, own_rows, width), tokens, expert_norm_gain,
        slot_of, place_of, expert_weight, expert_gate_weight, gate_head, expert_up_weight, up_extra, weight_rest,
        expert_down_weight,
    )


def solution(mesh):
    return jax.shard_map(
        on_device,
        mesh=mesh,
        in_specs=(
            P(("req", "tp"), None),
            P(),
            P(),
            P(None, "tp"),
            P(None, "tp"),
            P(None, "tp"),
            P("tp", None),
            P("req", "tp"),
            P("req", "tp"),
            P("req", None),
            P("req", None),
            P("req", None),
            P(),
            P("req", None, None),
            P("req", None, "tp"),
            P("req", None, "tp"),
            P("req", None),
            P("req", None),
            P("req", None, "tp"),
            P("req", None, "tp"),
            P("req", "tp", None),
        ),
        out_specs=P(("req", "tp"), None),
        check_vma=False,
    )
```
